32 devices in a mesh: rows: 8 (over z, y), seq: 4 (over x, core).
Axes of the slice: x: 2, y: 2, z: 4, core: 2. Of those that a mesh axis runs over, the one named last changes fastest.
Arguments:
- byte_ids: int32 [8, 2048], P('rows', 'seq'), may hold values from 0 to 255
- seg_ids: int32 [8, 2048], P('rows', 'seq'), may hold values from 0 to 15, never falling along the last dimension, each value on 1 to 1024 neighbouring positions
- row_len: int32 [8], P('rows'), may hold values from 256 to 2048, as said below
- embed_table: bfloat16 [256, 768], replicated, may hold values from -6 to 6
- conv_weight: bfloat16 [5, 768, 768], replicated, may hold values from -0.09375 to 0.09375
- conv_bias: float32 [768], replicated, may hold values from -3 to 3
- scorer: float32 [768], replicated, may hold values from -0.4375 to 0.4375
- calibration: float32 [4, 4], replicated, may hold values from -3 to 3
- cotangent: bfloat16 [8, 1024, 768], P('rows', 'seq'), may hold values from -6 to 6
Outputs:
- blocks: bfloat16 [8, 1024, 768], P('rows', 'seq')
- loss: float32 [], replicated
- grad_table: float32 [256, 768], replicated
- grad_conv: float32 [5, 768, 768], replicated
- grad_bias: float32 [768], replicated
- grad_scorer: float32 [768], replicated
- grad_calib: float32 [4, 4], replicated
The draws below stay inside these ranges and needn't reach their ends.
Inputs may be any that keep to these rules, and one draw needn't show every extreme that they name: `seg_ids`: within each row, segment numbers start at 0, never fall and rise by at most one from one byte to the next. `row_len`: each row holds real bytes first and padding after them.
All inputs are finite; a program needn't handle non-finite values.
Results may differ from the reference program's by a relative error of at most 0.015.
Values may be sent and summed in bfloat16 or wider, within the bound.
No kernel may reach another device: no remote copies, remote signals or barrier semaphores. Data moves between devices by JAX's collectives and lax.ppermute only.
A program may use at most 128 MiB of HBM per device.

```python
import math
import jax
import jax.numpy as jnp
import numpy as np
from jax import lax

D = 768
VOCAB = 256
KERNEL = 5
MAXB = 4
L = 2048
DOCS = 16
ROWS = 8


def draw_row_len(key, part):
    index = jnp.arange(ROWS, dtype=jnp.int32)
    floor_len = L // 8 + 3 * L // 4 * (ROWS - 1 - index) // ROWS
    drawn = jax.random.randint(key, (ROWS,), floor_len, floor_len + L // 8 + 1)
    drawn = jnp.minimum(drawn, L)
    drawn = jnp.where(index == 0, L, drawn)
    drawn = jnp.where(index == ROWS - 1, L // 8, drawn)
    return drawn.astype(jnp.int32)


def plant(array, own_key, smallest, top_value):
    extent = array.shape
    index_at = [jax.random.randint(jax.random.fold_in(own_key, axis), (), 0, extent[axis]) for axis in range(len(extent))]
    array = array.at[tuple(index_at)].set(smallest)
    longest = extent.index(max(extent))
    index_at[longest] = (index_at[longest] + 1) % extent[longest]
    return array.at[tuple(index_at)].set(top_value)


def shard_levels(rng, shape, split, smallest, high):
    def one(position, blocks):
        steps = jax.random.uniform(jax.random.fold_in(jax.random.fold_in(rng, 6), position), (blocks,), jnp.float32, smallest / len(split), high / len(split))
        return jnp.repeat(jnp.exp(steps), shape[position] // blocks).reshape((-1,) + (1,) * (len(shape) - position - 1))

    level = one(*split[0])
    for cut in split[1:]:
        level = level * one(*cut)
    return level


def cumulative_ranks(count, skew):
    weights = [(1 << 20) // math.isqrt(rank ** skew) + 1 for rank in range(1, count + 1)]
    spread = 1 + sum(weights) // (1 << 30)
    return np.cumsum(np.array([max(1, weight // spread) for weight in weights]))


def ranked(stream_key, dims, amount, skew):
    listing = cumulative_ranks(amount, skew)
    lot = jax.random.randint(jax.random.fold_in(stream_key, 1), dims, 0, int(listing[amount - 1]))
    grade = jnp.searchsorted(jnp.asarray(listing, jnp.int32), lot, side="right")
    return jax.random.permutation(jax.random.fold_in(stream_key, 2), amount)[grade].astype(jnp.int32)


def length_profile(count, total, bound, skew):
    loads = [(1 << 20) // math.isqrt(standing ** skew) + 1 for standing in range(2, count + 1)]
    spare, counts = total - bound - (count - 1), [1] * (count - 1)
    while spare > 0:
        free = [i for i in range(count - 1) if counts[i] < bound]
        pool, left = sum([loads[i] for i in free]), spare
        for i in free:
            more = min(bound - counts[i], max(1, left * loads[i] // pool), spare)
            counts[i] = counts[i] + more
            spare = spare - more
    return np.array([bound] + counts)


def uneven(stream_key, amount, total, limit, skew):
    if amount == 2:
        one = jax.random.randint(stream_key, (), max(1, total - limit), min(limit, total - 1) + 1)
        return jnp.stack([one, total - one])
    lengths = jnp.asarray(length_profile(amount, total, limit, skew), jnp.int32)
    couples = (amount - 1) // 2
    donor, taker = lengths[1:1 + 2 * couples:2], lengths[2:2 + 2 * couples:2]
    room = jnp.minimum(donor - 1, limit - taker)
    passed = jax.random.randint(jax.random.fold_in(stream_key, 1), (couples,), 0, 1 << 20) % (room + 1)
    lengths = lengths.at[1:1 + 2 * couples:2].set(donor - passed).at[2:2 + 2 * couples:2].set(taker + passed)
    return lengths[jax.random.permutation(jax.random.fold_in(stream_key, 2), amount)]


def gaussian(key, shape, deviation, most, pieces=(), held_as=jnp.bfloat16):
    values = deviation * jax.random.normal(key, shape, jnp.float32)
    if pieces:
        values = values * shard_levels(key, shape, pieces, -0.22, 0.18)
    return jnp.clip(values, -most, most).astype(held_as)


def setup_inputs(seed: int = 0) -> dict:
    seeds = jax.random.split(jax.random.key(seed), 10)
    return {
        "byte_ids": plant(ranked(seeds[0], (ROWS, L), VOCAB, 2), jax.random.fold_in(seeds[0], 3), 0, VOCAB - 1).astype(jnp.int32),
        "seg_ids": jax.vmap(lambda own: jnp.searchsorted(jnp.cumsum(uneven(own, DOCS, L, L // 2, 2)), jnp.arange(L), side="right"))(jax.random.split(seeds[1], ROWS)).reshape((ROWS, L)).astype(jnp.int32),
        "row_len": draw_row_len(jax.random.fold_in(seeds[9], 71), 0),
        "embed_table": gaussian(seeds[3], (VOCAB, D), 1.0, 6.0),
        "conv_weight": gaussian(seeds[4], (KERNEL, D, D), (KERNEL * D) ** -0.5, 0.09375),
        "conv_bias": gaussian(seeds[5], (D,), 0.5, 3.0, (), jnp.float32),
        "scorer": gaussian(seeds[6], (D,), (D // 4) ** -0.5, 0.4375, (), jnp.float32),
        "calibration": gaussian(seeds[7], (MAXB, MAXB), MAXB ** -0.5, 3.0, (), jnp.float32),
        "cotangent": gaussian(seeds[8], (ROWS, L // 2, D), 1.0, 6.0, ((0, 8), (1, 4))),
    }


@jax.custom_vjp
def low(v):
    return lax.optimization_barrier(v.astype(jnp.bfloat16)).astype(jnp.float32)

@jax.custom_vjp
def low_back(v):
    return v

def low_keep(v):
    return (low(v), None)

def low_pass(kept, grad):
    return (grad,)

def back_keep(v):
    return (v, None)

def back_low(kept, grad):
    return (low(grad),)
low.defvjp(low_keep, low_pass)
low_back.defvjp(back_keep, back_low)

def forward_rows(table_f, conv_f, bias_f, scorer_f, calib_f, byte_ids, seg_ids, real_mask):
    group_rows, length = byte_ids.shape
    precise = lax.Precision.HIGHEST
    embedded = low_back(table_f[byte_ids] * real_mask[:, :, None])
    padded_x = jnp.pad(embedded, ((0, 0), (KERNEL - 1, 0), (0, 0)))
    conv_full = bias_f
    for offset in range(KERNEL):
        conv_full = conv_full + jnp.einsum('rld,de->rle', padded_x[:, offset:offset + length], conv_f[offset], precision=precise)
    conv_low = low_back(low(conv_full))
    reach_len = MAXB - 1
    padded_y = jnp.pad(conv_low, ((0, 0), (reach_len, 0), (0, 0)))
    padded_seg = jnp.pad(seg_ids, ((0, 0), (reach_len, 0)), constant_values=-1)
    padded_mask = jnp.pad(real_mask, ((0, 0), (reach_len, 0)))
    running = jnp.zeros_like(conv_low)
    counted = jnp.zeros_like(real_mask)
    pooled_list = []
    for lag_idx in range(MAXB):
        begin = reach_len - lag_idx
        same_doc = (padded_seg[:, begin:begin + length] == seg_ids).astype(real_mask.dtype)
        valid = padded_mask[:, begin:begin + length] * real_mask * same_doc
        running = running + valid[:, :, None] * padded_y[:, begin:begin + length]
        counted = counted + valid
        pooled_list.append(running / jnp.maximum(counted, 1.0)[:, :, None])
    scores = jnp.stack([jnp.einsum('rld,d->rl', pooled, scorer_f, precision=precise) for pooled in pooled_list], axis=-1)
    logits = jnp.einsum('rlb,bc->rlc', scores, calib_f, precision=precise)
    probs = jax.nn.softmax(logits, axis=-1)
    mixed = probs[:, :, 0:1] * pooled_list[0]
    for size_idx in range(1, MAXB):
        mixed = mixed + probs[:, :, size_idx:size_idx + 1] * pooled_list[size_idx]
    blocks = lax.optimization_barrier(jnp.sum(mixed.reshape(group_rows, length // 2, 2, mixed.shape[-1]), axis=2)) * 0.5
    entropy = jnp.sum(real_mask * (jax.nn.logsumexp(logits, axis=-1) - lax.optimization_barrier(jnp.sum(probs * logits, axis=-1))))
    return (blocks, entropy)

def add_pair(first, second):
    return first + second

def reference(byte_ids, seg_ids, row_len, embed_table, conv_weight, conv_bias, scorer, calibration, cotangent):
    positions = jnp.arange(L, dtype=jnp.int32)
    real_mask = (positions[None, :] < row_len[:, None]).astype(jnp.float32)
    real_count = jnp.sum(row_len).astype(jnp.float32)
    params = (embed_table.astype(jnp.float32), conv_weight.astype(jnp.float32), conv_bias, scorer, calibration)
    group_rows = 1
    for candidate in range(1, max(1, 4096 // L) + 1):
        if ROWS % candidate == 0:
            group_rows = candidate
    group_count = ROWS // group_rows
    items = (byte_ids.reshape(group_count, group_rows, L), seg_ids.reshape(group_count, group_rows, L), real_mask.reshape(group_count, group_rows, L), cotangent.reshape(group_count, group_rows, L // 2, D))

    def one_group(carry, item):
        grads_sum, entropy_sum = carry
        ids_group, seg_group, mask_group, cot_group = item

        def objective(*weights):
            return forward_rows(*weights, ids_group, seg_group, mask_group)
        (blocks, entropy), pull = jax.vjp(objective, *params)
        grads = pull((cot_group.astype(jnp.float32), 1.0 / real_count))
        grads_sum = jax.tree.map(add_pair, grads_sum, grads)
        return ((grads_sum, entropy_sum + entropy), blocks.astype(jnp.bfloat16))
    init = (tuple((jnp.zeros_like(weight) for weight in params)), jnp.zeros((), jnp.float32))
    (grads, entropy), blocks = lax.scan(one_group, init, items)
    blocks = blocks.reshape(ROWS, L // 2, D)
    return (blocks, entropy / real_count, grads[0], grads[1], grads[2], grads[3], grads[4])
```

```python
import jax
import jax.numpy as jnp
import numpy as np
from jax import lax
from jax.experimental import pallas as pl
from jax.experimental.pallas import tpu as pltpu
from jax.sharding import PartitionSpec as P

AXES = ("rows", "seq")
BF = jnp.bfloat16
F32 = jnp.float32
HALO = 16
VMEM_LIMIT = 48 * 1024 * 1024


def dot_nn(a, b):
    return lax.dot_general(a, b, (((1,), (0,)), ((), ())), preferred_element_type=F32)


def dot_nt(a, b):
    return lax.dot_general(a, b, (((1,), (1,)), ((), ())), preferred_element_type=F32)


def dot_tn(a, b):
    return lax.dot_general(a, b, (((0,), (0,)), ((), ())), preferred_element_type=F32)


def split2(v):
    hi = v.astype(BF)
    return hi, (v - hi.astype(F32)).astype(BF)


def split3(v):
    hi = v.astype(BF)
    rest = v - hi.astype(F32)
    mid = rest.astype(BF)
    return hi, mid, (rest - mid.astype(F32)).astype(BF)


def call(kernel, outs, name, **kw):
    return pl.pallas_call(
        kernel,
        out_shape=outs,
        name=name,
        compiler_params=pltpu.CompilerParams(vmem_limit_bytes=VMEM_LIMIT),
        **kw,
    )


def vspec():
    return pl.BlockSpec(memory_space=pltpu.VMEM)


def sspec():
    return pl.BlockSpec(memory_space=pltpu.SMEM)


def shape(dims, dtype):
    return jax.ShapeDtypeStruct(dims, dtype)


def tap_kernel(table_ref, weight_ref, scorer_ref, hi_ref, lo_ref, q_ref):
    hi, lo = split2(dot_nn(table_ref[...], weight_ref[0]))
    hi_ref[0] = hi
    lo_ref[0] = lo

    @pl.when(pl.program_id(0) == 0)
    def _():
        s1, s2, s3 = split3(scorer_ref[...])
        row = lax.broadcasted_iota(jnp.int32, q_ref.shape, 0)
        pick = jnp.where(row == 0, s1.astype(F32), jnp.where(row == 1, s2.astype(F32), s3.astype(F32)))
        q_ref[...] = jnp.where(row < 3, pick, 0.0).astype(BF)


def roll(v, by):
    by = by % v.shape[1]
    return pltpu.roll(v, by, 1) if by else v


def local_kernel(
    info_ref, calib_ref, idk_ref, lane_ref, idt_ref, hi_ref, lo_ref, bias_ref, cot_ref, cot_next_ref,
    q_ref, blocks_ref, keep_ref, send_ref, ext_ref, y_ref, full_q_ref, oh_ref,
):
    taps, vocab, width = hi_ref.shape
    span = keep_ref.shape[0]
    half = width // 2
    own_blocks = span // 2
    rows_y = idk_ref.shape[0]
    lanes = y_ref.shape[0]
    sizes = calib_ref.shape[0]
    value = lax.broadcasted_iota(jnp.int32, (rows_y, vocab), 1).astype(F32)
    acc = jnp.broadcast_to(bias_ref[...], (rows_y, width))
    for k in range(taps):
        one_hot = jnp.where(idk_ref[:, k : k + 1] == value, 1.0, 0.0).astype(BF)
        oh_ref[k] = one_hot
        acc = acc + (dot_nn(one_hot, hi_ref[k]) + dot_nn(one_hot, lo_ref[k]))
    y = acc.astype(BF)
    front = span + HALO
    y_ref[0:front] = y[0:front]
    y_ref[front : lanes - HALO] = jnp.zeros((lanes - HALO - front, width), BF)
    y_ref[lanes - HALO : lanes] = y[front : front + HALO]
    full_q_ref[0:own_blocks] = cot_ref[...]
    full_q_ref[own_blocks : own_blocks + HALO] = cot_next_ref[...]
    full_q_ref[own_blocks + HALO : own_blocks + 2 * HALO] = q_ref[...]
    tail = own_blocks + HALO
    q_rows = own_blocks + 2 * HALO
    dots = dot_nt(full_q_ref[...], y_ref[...])
    u = dots[tail : tail + 1] + dots[tail + 1 : tail + 2] + dots[tail + 2 : tail + 3]

    pos = lax.broadcasted_iota(jnp.int32, (1, lanes), 1)
    own = jnp.where(pos < span, 1.0, 0.0)
    seg = lane_ref[0:1]
    mask = lane_ref[1:2]
    line = lax.broadcasted_iota(jnp.int32, (q_rows, lanes), 0)
    valid, match, grads = [], [], []
    for d in range(sizes):
        valid.append(mask * roll(mask, d) * jnp.where(seg == roll(seg, d), 1.0, 0.0))
        ahead = jnp.where(pos + d >= lanes, pos + d - lanes, pos + d)
        block = jnp.where(ahead < front, lax.shift_right_logical(ahead, 1), -1)
        match.append(line == block)
        picked = jnp.sum(jnp.where(match[d], dots, 0.0), axis=0, keepdims=True)
        grads.append(0.5 * roll(picked, d))
    counted, inv, scores, dprobs = 0.0, [], [], []
    run_u, run_g = 0.0, 0.0
    for d in range(sizes):
        counted = counted + valid[d]
        inv.append(1.0 / jnp.maximum(counted, 1.0))
        run_u = run_u + valid[d] * roll(u, d)
        run_g = run_g + valid[d] * grads[d]
        scores.append(run_u * inv[d])
        dprobs.append(run_g * inv[d])
    logits = [sum(scores[b] * calib_ref[b, c] for b in range(sizes)) for c in range(sizes)]
    top = logits[0]
    for c in range(1, sizes):
        top = jnp.maximum(top, logits[c])
    powers = [jnp.exp(v - top) for v in logits]
    total = sum(powers)
    probs = [v / total for v in powers]
    lse = top + jnp.log(total)
    mean_logit = sum(p * v for p, v in zip(probs, logits))
    mean_grad = sum(p * v for p, v in zip(probs, dprobs))
    entropy = own * mask * (lse - mean_logit)
    parts = [
        [p * (v - mean_grad) for p, v in zip(probs, dprobs)],
        [mask * p * (v - mean_logit) for p, v in zip(probs, logits)],
    ]
    alpha, later = [None] * sizes, 0.0
    for d in reversed(range(sizes)):
        later = later + probs[d] * inv[d]
        alpha[d] = valid[d] * later
    gammas, rhos, calibs = [], [], []
    for part in parts:
        dscores = [sum(part[c] * calib_ref[b, c] for c in range(sizes)) for b in range(sizes)]
        later, gamma, rho = 0.0, 0.0, 0.0
        for d in reversed(range(sizes)):
            later = later + inv[d] * dscores[d]
            beta = valid[d] * later
            gamma = gamma + roll(beta, -d)
            rho = rho + roll(beta * own, -d)
        gammas.append(gamma)
        rhos.append(rho)
        calibs.append([[jnp.sum(own * scores[b] * part[c], axis=1, keepdims=True) for c in range(sizes)] for b in range(sizes)])
    band = jnp.where((line >= tail) & (line < tail + 3), gammas[0], 0.0)
    for d in range(sizes):
        band = band + jnp.where(match[d], 0.5 * roll(alpha[d], -d), 0.0)
    band_hi, band_lo = split2(band)
    mixed = dot_nn(band_hi[0:own_blocks], y_ref[...]) + dot_nn(band_lo[0:own_blocks], y_ref[...])
    blocks_ref[...] = mixed.astype(BF)
    dy = dot_tn(band_hi[:, 0:span], full_q_ref[...]) + dot_tn(band_lo[:, 0:span], full_q_ref[...])
    dy = dy.astype(BF)
    left, right = dy[:, 0:half], dy[:, half:width]
    upper = info_ref[0] == 1
    keep_ref[...] = jnp.where(upper, right, left)
    send_ref[0:span] = jnp.where(upper, left, right)
    grad_bias = jnp.sum(dy.astype(F32), axis=0, keepdims=True)

    row8 = lax.broadcasted_iota(jnp.int32, (16, lanes), 0)
    stack = jnp.zeros((16, lanes), F32)
    pieces = split3(rhos[0]) + split3(rhos[1]) + split3(gammas[1] * own)
    for i, piece in enumerate(pieces):
        stack = jnp.where(row8 == i, piece.astype(F32), stack)
    stack = stack.astype(BF)
    by_y = dot_nn(stack, y_ref[...])
    grad_scorer = [by_y[3 * i : 3 * i + 1] + by_y[3 * i + 1 : 3 * i + 2] + by_y[3 * i + 2 : 3 * i + 3] for i in range(2)]
    ext_ref[...] = jnp.zeros(ext_ref.shape, F32)
    for i, row in enumerate(grad_scorer + [grad_bias]):
        ext_ref[2 * i : 2 * i + 1] = row[:, 0:half]
        ext_ref[2 * i + 1 : 2 * i + 2] = row[:, half:width]
    for k in range(taps):
        by_tap = dot_nn(stack[:, 0:span], oh_ref[k, 0:span])
        ext_ref[6 + k : 7 + k, 0:vocab] = by_tap[6:7] + by_tap[7:8] + by_tap[8:9]
    spot = lax.broadcasted_iota(jnp.int32, (1, half), 1)
    misc = jnp.zeros((1, half), F32)
    sums = [calibs[i][b][c] for i in range(2) for b in range(sizes) for c in range(sizes)]
    sums.append(jnp.sum(entropy, axis=1, keepdims=True))
    sums.append(jnp.sum(own * mask, axis=1, keepdims=True))
    sums.append(jnp.sum(own * gammas[1], axis=1, keepdims=True))
    for i, one in enumerate(sums):
        misc = jnp.where(spot == i, one, misc)
    ext_ref[11:12] = misc
    ext_hi, ext_lo = split2(ext_ref[...])
    send_ref[span : span + 16] = ext_hi
    send_ref[span + 16 : span + 32] = ext_lo
    ids = idt_ref[...]
    send_ref[span + 32 : span + 48] = jnp.concatenate([ids, jnp.zeros((16, half - ids.shape[1]), BF)], axis=1)


def joined(ext_ref):
    hi, lo = split2(ext_ref[...])
    return hi.astype(F32) + lo.astype(F32)


def pair(ref, at):
    return ref[at : at + 16].astype(F32) + ref[at + 16 : at + 32].astype(F32)


def local_value(shape_, dim, info_ref, vocab):
    slot = lax.broadcasted_iota(jnp.int32, shape_, dim)
    mine = jnp.where(slot < vocab // 2, info_ref[1], info_ref[2])
    return jnp.bitwise_xor(slot, mine)


def table_kernel(info_ref, keep_ref, idt_ref, got_ref, ext_ref, a_keep, a_send, b_keep, b_send, ext_out):
    span, half = keep_ref.shape
    taps, quarter, _ = a_keep.shape
    vocab = 4 * quarter
    value = local_value((vocab, 1), 0, info_ref, vocab).astype(F32)
    mine = idt_ref[...].astype(F32)
    theirs = got_ref[span + 32 : span + 48].astype(F32)
    wide = mine.shape[1]
    for k in range(taps):
        acc = None
        for i in range(span // wide):
            for ids, grad in ((mine, keep_ref), (theirs, got_ref)):
                row = ids[2 * k + i : 2 * k + i + 1, 0:wide]
                one_hot = jnp.where(row == value, 1.0, 0.0).astype(BF)
                term = dot_nn(one_hot, grad[i * wide : (i + 1) * wide])
                acc = term if acc is None else acc + term
        a_keep[k] = acc[0:quarter]
        a_send[k * quarter : (k + 1) * quarter] = acc[quarter : 2 * quarter].astype(BF)
        b_keep[k] = acc[2 * quarter : 3 * quarter]
        b_send[k * quarter : (k + 1) * quarter] = acc[3 * quarter : 4 * quarter].astype(BF)
    ext = joined(ext_ref) + pair(got_ref, span)
    ext_out[...] = ext
    hi, lo = split2(ext)
    a_send[taps * quarter : taps * quarter + 16] = hi
    a_send[taps * quarter + 16 : taps * quarter + 32] = lo


def second_kernel(a_in, b_in, a_got, b_got, ext_ref, a_keep, a_send, b_keep, b_send, ext_out):
    taps, rows, _ = a_in.shape
    part = rows // 2
    for src, got, keep, send in ((a_in, a_got, a_keep, a_send), (b_in, b_got, b_keep, b_send)):
        for k in range(taps):
            total = src[k] + got[k * rows : (k + 1) * rows].astype(F32)
            keep[k] = total[0:part]
            send[k * part : (k + 1) * part] = total[part:rows].astype(BF)
    ext = joined(ext_ref) + pair(a_got, taps * rows)
    ext_out[...] = ext
    hi, lo = split2(ext)
    a_send[taps * part : taps * part + 16] = hi
    a_send[taps * part + 16 : taps * part + 32] = lo


def third_kernel(a_in, b_in, a_got, b_got, ext_ref, keep, ext_out, *sends):
    taps, rows, _ = a_in.shape
    peers = len(sends)
    part = rows // (peers + 1)
    ext = joined(ext_ref) + pair(a_got, taps * rows)
    ext_out[...] = ext
    hi, lo = split2(ext)
    groups = 2 * taps
    pieces = [[] for _ in range(peers + 1)]
    for src, got in ((a_in, a_got), (b_in, b_got)):
        for k in range(taps):
            total = src[k] + got[k * rows : (k + 1) * rows].astype(F32)
            for t in range(peers + 1):
                pieces[t].append(total[t * part : (t + 1) * part])
    for t in range(peers + 1):
        block = jnp.concatenate(pieces[t], axis=0)
        if t == 0:
            keep[...] = block
        else:
            send = sends[t - 1]
            send[0 : groups * part] = block.astype(BF)
            send[groups * part : groups * part + 16] = hi
            send[groups * part + 16 : groups * part + 32] = lo


def tree_sum(items):
    while len(items) > 1:
        items = [items[i] + items[i + 1] for i in range(0, len(items), 2)]
    return items[0]


def shard_kernel(info_ref, keep, ext_ref, scorer_ref, *refs):
    gots, (shard, small) = refs[:-2], refs[-2:]
    size = keep.shape[0]
    half = keep.shape[1]
    vocab = 256
    taps = 5
    part = size // (2 * taps)
    ext = tree_sum([joined(ext_ref)] + [pair(g, size) for g in gots])
    total = tree_sum([keep[...]] + [g[0:size].astype(F32) for g in gots])
    spot = lax.broadcasted_iota(jnp.int32, (1, half), 1)
    misc = ext[11:12]

    def one(i):
        return jnp.sum(jnp.where(spot == i, misc, 0.0), axis=1, keepdims=True)

    count = one(33)
    scorer = scorer_ref[...]
    upper = info_ref[0] == 1
    mine = jnp.where(upper, scorer[1:2], scorer[0:1])
    step = lax.broadcasted_iota(jnp.int32, (part, vocab), 0)
    lane = lax.broadcasted_iota(jnp.int32, (part, vocab), 1)
    for g in range(2):
        first = info_ref[1 + g]
        hit = lane == first + step
        for k in range(taps):
            column = jnp.sum(jnp.where(hit, ext[6 + k : 7 + k, 0:vocab], 0.0), axis=1, keepdims=True)
            at = (g * taps + k) * part
            piece = total[at : at + part] - (column / count) * mine
            shard[at : at + part] = piece.astype(BF)
    for h in range(2):
        small[h : h + 1] = ext[h : h + 1] - ext[2 + h : 3 + h] / count
        small[2 + h : 3 + h] = ext[4 + h : 5 + h] - (one(34) / count) * scorer[h : h + 1]
    moved = roll(misc, -16)
    small[4:5] = jnp.where(spot < 16, misc - moved / count, misc / count)
    small[5:8] = jnp.zeros((3, half), F32)


def final_kernel(
    info_ref, col_ref, early_ref, a_ref, b_ref, table_t_ref, weight_ref, conv_in, table_in,
    conv_ref, table_ref, perm_ref,
):
    k = pl.program_id(0)
    vocab = table_ref.shape[0]

    @pl.when(k == 0)
    def _():
        value = local_value((1, vocab), 1, info_ref, vocab)
        natural = lax.broadcasted_iota(jnp.int32, (vocab, vocab), 0)
        perm_ref[...] = jnp.where(natural == value, 1.0, 0.0).astype(BF)
        if table_in is None:
            table_ref[...] = jnp.zeros(table_ref.shape, F32)
        else:
            table_ref[...] = table_in[...]

    local = jnp.concatenate([early_ref[0, 0], a_ref[0], early_ref[1, 0], b_ref[0]], axis=0)
    rows = dot_nn(perm_ref[...], local).astype(BF)
    conv_ref[0] = dot_nn(table_t_ref[...], rows)
    table_ref[...] += dot_nt(rows, weight_ref[0])


def finish(info, col, early, a, b, table_t, weight, conv_in=None, table_in=None):
    taps, width, _ = weight.shape
    vocab = table_t.shape[1]
    half = width // 2
    quarter = vocab // 4
    specs = [
        pl.BlockSpec((2, 1, quarter, half), lambda k, info, col: (0, k, 0, 0)),
        pl.BlockSpec((1, quarter, half), lambda k, info, col: (k, 0, 0)),
        pl.BlockSpec((1, quarter, half), lambda k, info, col: (k, 0, 0)),
        pl.BlockSpec((width, vocab), lambda k, info, col: (0, 0)),
        pl.BlockSpec((1, width, half), lambda k, info, col: (k, 0, col[0])),
    ]
    args = [early, a, b, table_t, weight]
    kernel = final_kernel
    aliases = {}
    if conv_in is None:

        def kernel(info_ref, col_ref, e, a, b, t, w, conv_ref, table_ref, perm_ref):
            final_kernel(info_ref, col_ref, e, a, b, t, w, None, None, conv_ref, table_ref, perm_ref)

    else:
        specs += [pl.BlockSpec(memory_space=pl.ANY), pl.BlockSpec((vocab, width), lambda k, info, col: (0, 0))]
        args += [conv_in, table_in]
        aliases = {7: 0}
    return pl.pallas_call(
        kernel,
        out_shape=(shape((taps, width, width), F32), shape((vocab, width), F32)),
        grid_spec=pltpu.PrefetchScalarGridSpec(
            num_scalar_prefetch=2,
            grid=(taps,),
            in_specs=specs,
            out_specs=(
                pl.BlockSpec((1, width, half), lambda k, info, col: (k, 0, col[0])),
                pl.BlockSpec((vocab, width), lambda k, info, col: (0, 0)),
            ),
            scratch_shapes=[pltpu.VMEM((vocab, vocab), BF)],
        ),
        input_output_aliases=aliases,
        name="finish_first" if conv_in is None else "finish_second",
        compiler_params=pltpu.CompilerParams(vmem_limit_bytes=VMEM_LIMIT),
    )(info, col, *args)


def neighbour(shard, axis, by):
    length = lax.axis_size(axis)
    return lax.ppermute(shard, axis, [(i, i + by) for i in range(length) if 0 <= i + by < length])


def swap(shard, flip, count):
    return lax.ppermute(shard, AXES, [(i, i ^ flip) for i in range(count)])


def body(
    byte_ids, seg_ids, row_len, embed_table, conv_weight, conv_bias, scorer, calibration, cotangent
):
    row_count, span = byte_ids.shape
    vocab, width = embed_table.shape
    taps = conv_weight.shape[0]
    half = width // 2
    quarter = vocab // 4
    seq_size = lax.axis_size("seq")
    count = lax.axis_size("rows") * seq_size
    depth = count // 8
    assert row_count == 1 and vocab == 256 and taps == 5 and calibration.shape == (4, 4)
    assert seq_size % 2 == 0 and depth >= 1 and quarter // 2 % depth == 0
    part = quarter // 2 // depth
    number = np.arange(count)
    x_bit, y_bit, rest = (number >> 1) & 1, (number >> 2) & 1, number >> 3
    a_mine = x_bit * quarter + y_bit * (quarter // 2) + rest * part
    b_mine = vocab // 2 + y_bit * quarter + x_bit * (quarter // 2) + rest * part
    facts = np.stack([number & 1, a_mine, b_mine - vocab // 2, 1 - (number & 1)], axis=1).astype(np.int32)
    device = lax.axis_index("rows") * seq_size + lax.axis_index("seq")
    info = lax.dynamic_slice(jnp.asarray(facts), (device, 0), (1, 4)).reshape(4)
    shard_info = info + jnp.asarray(np.array([0, 0, vocab // 2, 0], np.int32))

    ids = byte_ids[0].astype(F32)
    segs = seg_ids[0].astype(F32)
    cot = cotangent[0]
    to_right = jnp.stack([ids[span - HALO :], segs[span - HALO :]]).astype(BF)
    to_left = jnp.concatenate(
        [cot[:HALO], jnp.pad(jnp.stack([ids[:HALO], segs[:HALO]]).astype(BF), ((0, HALO - 2), (0, width - HALO)))]
    )
    from_left = neighbour(to_right, "seq", 1)
    from_right = neighbour(to_left, "seq", -1)

    hi, lo, q_rows = pl.pallas_call(
        tap_kernel,
        out_shape=(shape((taps, vocab, width), BF), shape((taps, vocab, width), BF), shape((16, width), BF)),
        grid=(taps,),
        in_specs=[
            pl.BlockSpec((vocab, width), lambda k: (0, 0)),
            pl.BlockSpec((1, width, width), lambda k: (k, 0, 0)),
            pl.BlockSpec((1, width), lambda k: (0, 0)),
        ],
        out_specs=(
            pl.BlockSpec((1, vocab, width), lambda k: (k, 0, 0)),
            pl.BlockSpec((1, vocab, width), lambda k: (k, 0, 0)),
            pl.BlockSpec((16, width), lambda k: (0, 0)),
        ),
        name="taps",
        compiler_params=pltpu.CompilerParams(vmem_limit_bytes=VMEM_LIMIT),
    )(embed_table, conv_weight, scorer[None])

    start = lax.axis_index("seq") * span
    near_left = from_left.astype(F32)
    near_right = from_right[HALO : HALO + 2, :HALO].astype(F32)
    line_ids = jnp.concatenate([near_left[0], ids, near_right[0]])
    line_segs = jnp.concatenate([near_left[1], segs, near_right[1]])
    line_pos = start - HALO + jnp.arange(span + 2 * HALO, dtype=jnp.int32)
    real = (line_pos >= 0) & (line_pos < row_len[0])
    known = jnp.where(real, line_ids, -1.0)
    padded = jnp.concatenate([jnp.full((taps - 1,), -1.0, F32), known])
    shifted = [padded[k : k + span + 2 * HALO] for k in range(taps)]
    idk = jnp.stack([jnp.concatenate([s[HALO:], s[:HALO]]) for s in shifted] + [jnp.zeros((span + 2 * HALO,), F32)] * (8 - taps), axis=1)
    idt = jnp.stack([s[HALO : HALO + span] for s in shifted]).astype(BF).reshape(2 * taps, span // 2)
    idt = jnp.pad(idt, ((0, 16 - 2 * taps), (0, 0)))
    lanes = span + 128
    gap = jnp.zeros((lanes - span - 2 * HALO,), F32)

    def lane_row(v):
        return jnp.concatenate([v[HALO:], gap, v[:HALO]])

    lane = jnp.stack([lane_row(line_segs), lane_row(real.astype(F32))] + [jnp.zeros((lanes,), F32)] * 6)

    blocks, keep, send, ext = call(
        local_kernel,
        (
            shape((span // 2, width), BF),
            shape((span, half), BF),
            shape((span + 48, half), BF),
            shape((16, half), F32),
        ),
        "local",
        in_specs=[sspec(), sspec()] + [vspec()] * 9,
        out_specs=(vspec(),) * 4,
        scratch_shapes=[
            pltpu.VMEM((lanes, width), BF),
            pltpu.VMEM((span // 2 + 2 * HALO, width), BF),
            pltpu.VMEM((taps, span + 2 * HALO, vocab), BF),
        ],
    )(info, calibration, idk, lane, idt, hi, lo, conv_bias[None], cot, from_right[:HALO], q_rows)

    got = swap(send, 1, count)
    a_keep, a_send, b_keep, b_send, ext = call(
        table_kernel,
        (
            shape((taps, quarter, half), F32),
            shape((taps * quarter + 32, half), BF),
            shape((taps, quarter, half), F32),
            shape((taps * quarter, half), BF),
            shape((16, half), F32),
        ),
        "by_value",
        in_specs=[sspec()] + [vspec()] * 4,
        out_specs=(vspec(),) * 5,
    )(info, keep, idt, got, ext)

    a_got, b_got = swap(a_send, 2, count), swap(b_send, 4, count)
    eighth = quarter // 2
    a_keep, a_send, b_keep, b_send, ext = call(
        second_kernel,
        (
            shape((taps, eighth, half), F32),
            shape((taps * eighth + 32, half), BF),
            shape((taps, eighth, half), F32),
            shape((taps * eighth, half), BF),
            shape((16, half), F32),
        ),
        "second",
        in_specs=[vspec()] * 5,
        out_specs=(vspec(),) * 5,
    )(a_keep, b_keep, a_got, b_got, ext)

    a_got, b_got = swap(a_send, 4, count), swap(b_send, 2, count)
    size = 2 * taps * part
    outs = call(
        third_kernel,
        (shape((size, half), F32), shape((16, half), F32)) + (shape((size + 32, half), BF),) * (depth - 1),
        "third",
        in_specs=[vspec()] * 5,
        out_specs=(vspec(),) * (depth + 1),
    )(a_keep, b_keep, a_got, b_got, ext)
    mine, ext, sends = outs[0], outs[1], outs[2:]
    gots = [swap(s, 8 * (t + 1), count) for t, s in enumerate(sends)]
    shard, small = call(
        shard_kernel,
        (shape((size, half), BF), shape((8, half), F32)),
        "shard",
        in_specs=[sspec()] + [vspec()] * (3 + len(gots)),
        out_specs=(vspec(),) * 2,
    )(shard_info, mine, ext, scorer.reshape(2, half), *gots)

    gathered = [shard] + [swap(shard, 8 * t, count) for t in range(1, depth)]
    ab = jnp.concatenate([g.reshape(2, taps, part, half) for g in gathered], axis=2)
    a_got, b_got = swap(ab[0], 4, count), swap(ab[1], 2, count)
    early = jnp.concatenate([ab, jnp.stack([a_got, b_got])], axis=2)
    a_got, b_got = swap(early[0], 2, count), swap(early[1], 4, count)
    early_far = swap(early, 1, count)
    a_far, b_far = swap(a_got, 1, count), swap(b_got, 1, count)

    table_t = embed_table.T
    conv, table = finish(info, info[0:1], early, a_got, b_got, table_t, conv_weight)
    conv, table = finish(info, info[3:4], early_far, a_far, b_far, table_t, conv_weight, conv, table)
    grad_scorer = small[0:2].reshape(width)
    grad_bias = small[2:4].reshape(width)
    grad_calib = small[4, 0:16].reshape(4, 4)
    loss = small[4, 32]
    return (blocks[None], loss, table, conv, grad_bias, grad_scorer, grad_calib)


def solution(mesh):
    return jax.shard_map(
        body,
        mesh=mesh,
        in_specs=(
            P("rows", "seq"),
            P("rows", "seq"),
            P("rows"),
            P(),
            P(),
            P(),
            P(),
            P(),
            P("rows", "seq", None),
        ),
        out_specs=(P("rows", "seq", None), P(), P(), P(), P(), P(), P()),
        check_vma=False,
    )
```

```python
import functools

import jax
import jax.numpy as jnp
from jax import lax
from jax.experimental import pallas as pl
from jax.experimental.pallas import tpu as pltpu
from jax.sharding import PartitionSpec as P

AXES = ("rows", "seq")
BF = jnp.bfloat16
F32 = jnp.float32
HALO = 16
VMEM_LIMIT = 48 * 1024 * 1024


def dot_nn(a, b):
    return lax.dot_general(a, b, (((1,), (0,)), ((), ())), preferred_element_type=F32)


def dot_nt(a, b):
    return lax.dot_general(a, b, (((1,), (1,)), ((), ())), preferred_element_type=F32)


def dot_tn(a, b):
    return lax.dot_general(a, b, (((0,), (0,)), ((), ())), preferred_element_type=F32)


def split2(v):
    hi = v.astype(BF)
    return hi, (v - hi.astype(F32)).astype(BF)


def split3(v):
    hi = v.astype(BF)
    rest = v - hi.astype(F32)
    mid = rest.astype(BF)
    return hi, mid, (rest - mid.astype(F32)).astype(BF)


def call(kernel, outs, name, **kw):
    return pl.pallas_call(
        kernel,
        out_shape=outs,
        name=name,
        compiler_params=pltpu.CompilerParams(vmem_limit_bytes=VMEM_LIMIT),
        **kw,
    )


def vspec():
    return pl.BlockSpec(memory_space=pltpu.VMEM)


def sspec():
    return pl.BlockSpec(memory_space=pltpu.SMEM)


def shape(dims, dtype):
    return jax.ShapeDtypeStruct(dims, dtype)


def place(seq_size, quarter, part):
    device = lax.axis_index("rows") * seq_size + lax.axis_index("seq")
    x_bit = (device >> 1) & 1
    y_bit = (device >> 2) & 1
    rest = (device >> 3) * part
    a_mine = x_bit * quarter + y_bit * (quarter // 2) + rest
    b_mine = y_bit * quarter + x_bit * (quarter // 2) + rest
    return (device & 1) == 1, a_mine, b_mine


def pack_kernel(ids_ref, seg_ref, cot_ref, right_ref, left_ref):
    span = ids_ref.shape[1]
    width = cot_ref.shape[2]
    row = lax.broadcasted_iota(jnp.int32, (HALO, span), 0)
    ids = ids_ref[...].astype(F32)
    segs = seg_ref[...].astype(F32)
    both = jnp.where(row == 0, ids, jnp.where(row == 1, segs, 0.0)).astype(BF)
    right_ref[...] = both
    left_ref[0:HALO] = cot_ref[0]
    left_ref[HALO : 2 * HALO, 0:span] = both
    left_ref[HALO : 2 * HALO, span:width] = jnp.zeros((HALO, width - span), BF)


def tap_kernel(table_ref, weight_ref, scorer_ref, hi_ref, lo_ref, q_ref):
    hi, lo = split2(dot_nn(table_ref[...], weight_ref[0]))
    hi_ref[...] = hi
    lo_ref[...] = lo

    @pl.when(pl.program_id(0) == 0)
    def _():
        s1, s2, s3 = split3(scorer_ref[...].reshape(1, q_ref.shape[1]))
        row = lax.broadcasted_iota(jnp.int32, q_ref.shape, 0)
        pick = jnp.where(row == 0, s1.astype(F32), jnp.where(row == 1, s2.astype(F32), s3.astype(F32)))
        q_ref[...] = jnp.where(row < 3, pick, 0.0).astype(BF)


def roll(v, by):
    by = by % v.shape[1]
    return pltpu.roll(v, by, 1) if by else v


def local_kernel(
    row_len_ref, calib_ref, ids_ref, seg_ref, from_left_ref, from_right_ref, hi_ref, lo_ref, bias_ref, cot_ref,
    q_ref, blocks_ref, keep_ref, send_ref, ext_ref, idt_ref, y_ref, full_q_ref, oh_ref, *, seq_size, taps,
):
    span = keep_ref.shape[0]
    width = hi_ref.shape[1]
    vocab = hi_ref.shape[0] // taps
    half = width // 2
    own_blocks = span // 2
    lanes = y_ref.shape[0]
    sizes = calib_ref.shape[0]
    front = span + HALO
    upper = place(seq_size, 1, 1)[0]
    spare = lax.broadcasted_iota(jnp.int32, (1, lanes - span), 1)

    def line_up(own, at):
        near_right = from_right_ref[HALO : 2 * HALO, 0 : lanes - span].astype(F32)[at : at + 1]
        near_left = from_left_ref[:, 2 * span - lanes : span].astype(F32)[at : at + 1]
        rest = jnp.where(spare < HALO, near_right, jnp.where(spare >= lanes - span - HALO, near_left, 0.0))
        return jnp.concatenate([own.astype(F32), rest], axis=1)

    pos = lax.broadcasted_iota(jnp.int32, (1, lanes), 1)
    own = jnp.where(pos < span, 1.0, 0.0)
    place_in_row = lax.axis_index("seq") * span + jnp.where(pos < front, pos, pos - lanes)
    near = (pos < front) | (pos >= lanes - HALO)
    mask = jnp.where(near & (place_in_row >= 0) & (place_in_row < row_len_ref[0]), 1.0, 0.0)
    seg = line_up(seg_ref[...], 1)
    known = jnp.where(mask > 0.5, line_up(ids_ref[...], 0), -1.0)
    value = lax.broadcasted_iota(jnp.int32, (vocab, 1), 0).astype(F32)
    row16 = lax.broadcasted_iota(jnp.int32, (16, span // 2), 0)
    idt = jnp.zeros((16, span // 2), F32)
    for k in range(taps):
        moved = roll(known, taps - 1 - k)
        oh_ref[k * vocab : (k + 1) * vocab] = jnp.where(moved == value, 1.0, 0.0).astype(BF)
        for i in range(2):
            idt = jnp.where(row16 == 2 * k + i, moved[:, i * (span // 2) : (i + 1) * (span // 2)], idt)
    idt = idt.astype(BF)
    idt_ref[...] = idt
    y = dot_tn(oh_ref[...], hi_ref[...]) + dot_tn(oh_ref[...], lo_ref[...])
    y_ref[...] = (y + bias_ref[...].reshape(1, width)).astype(BF)
    full_q_ref[0:own_blocks] = cot_ref[0]
    full_q_ref[own_blocks : own_blocks + HALO] = from_right_ref[0:HALO]
    full_q_ref[own_blocks + HALO : own_blocks + 2 * HALO] = q_ref[...]
    tail = own_blocks + HALO
    q_rows = own_blocks + 2 * HALO
    dots = dot_nt(full_q_ref[...], y_ref[...])
    u = dots[tail : tail + 1] + dots[tail + 1 : tail + 2] + dots[tail + 2 : tail + 3]

    line = lax.broadcasted_iota(jnp.int32, (q_rows, lanes), 0)
    valid, match, grads = [], [], []
    for d in range(sizes):
        valid.append(mask * roll(mask, d) * jnp.where(seg == roll(seg, d), 1.0, 0.0))
        ahead = jnp.where(pos + d >= lanes, pos + d - lanes, pos + d)
        block = jnp.where(ahead < front, lax.shift_right_logical(ahead, 1), -1)
        match.append(line == block)
        picked = jnp.sum(jnp.where(match[d], dots, 0.0), axis=0, keepdims=True)
        grads.append(0.5 * roll(picked, d))
    counted, inv, scores, dprobs = 0.0, [], [], []
    run_u, run_g = 0.0, 0.0
    for d in range(sizes):
        counted = counted + valid[d]
        inv.append(1.0 / jnp.maximum(counted, 1.0))
        run_u = run_u + valid[d] * roll(u, d)
        run_g = run_g + valid[d] * grads[d]
        scores.append(run_u * inv[d])
        dprobs.append(run_g * inv[d])
    logits = [sum(scores[b] * calib_ref[b, c] for b in range(sizes)) for c in range(sizes)]
    top = logits[0]
    for c in range(1, sizes):
        top = jnp.maximum(top, logits[c])
    powers = [jnp.exp(v - top) for v in logits]
    total = sum(powers)
    probs = [v / total for v in powers]
    lse = top + jnp.log(total)
    mean_logit = sum(p * v for p, v in zip(probs, logits))
    mean_grad = sum(p * v for p, v in zip(probs, dprobs))
    entropy = own * mask * (lse - mean_logit)
    parts = [
        [p * (v - mean_grad) for p, v in zip(probs, dprobs)],
        [mask * p * (v - mean_logit) for p, v in zip(probs, logits)],
    ]
    alpha, later = [None] * sizes, 0.0
    for d in reversed(range(sizes)):
        later = later + probs[d] * inv[d]
        alpha[d] = valid[d] * later
    gammas, rhos, calibs = [], [], []
    for part in parts:
        dscores = [sum(part[c] * calib_ref[b, c] for c in range(sizes)) for b in range(sizes)]
        later, gamma, rho = 0.0, 0.0, 0.0
        for d in reversed(range(sizes)):
            later = later + inv[d] * dscores[d]
            beta = valid[d] * later
            gamma = gamma + roll(beta, -d)
            rho = rho + roll(beta * own, -d)
        gammas.append(gamma)
        rhos.append(rho)
        calibs.append([[jnp.sum(own * scores[b] * part[c], axis=1, keepdims=True) for c in range(sizes)] for b in range(sizes)])
    band = jnp.where((line >= tail) & (line < tail + 3), gammas[0], 0.0)
    for d in range(sizes):
        band = band + jnp.where(match[d], 0.5 * roll(alpha[d], -d), 0.0)
    band_hi, band_lo = split2(band)
    mixed = dot_nn(band_hi[0:own_blocks], y_ref[...]) + dot_nn(band_lo[0:own_blocks], y_ref[...])
    blocks_ref[0] = mixed.astype(BF)
    dy = dot_tn(band_hi[:, 0:span], full_q_ref[...]) + dot_tn(band_lo[:, 0:span], full_q_ref[...])
    dy = dy.astype(BF)
    left, right = dy[:, 0:half], dy[:, half:width]
    keep_ref[...] = jnp.where(upper, right, left)
    send_ref[0:span] = jnp.where(upper, left, right)
    grad_bias = jnp.sum(dy.astype(F32), axis=0, keepdims=True)

    row8 = lax.broadcasted_iota(jnp.int32, (16, lanes), 0)
    stack = jnp.zeros((16, lanes), F32)
    pieces = split3(rhos[0]) + split3(rhos[1]) + split3(gammas[1] * own)
    for i, piece in enumerate(pieces):
        stack = jnp.where(row8 == i, piece.astype(F32), stack)
    stack = stack.astype(BF)
    by_y = dot_nn(stack, y_ref[...])
    grad_scorer = [by_y[3 * i : 3 * i + 1] + by_y[3 * i + 1 : 3 * i + 2] + by_y[3 * i + 2 : 3 * i + 3] for i in range(2)]
    ext_ref[...] = jnp.zeros(ext_ref.shape, F32)
    for i, row in enumerate(grad_scorer + [grad_bias]):
        ext_ref[2 * i : 2 * i + 1] = row[:, 0:half]
        ext_ref[2 * i + 1 : 2 * i + 2] = row[:, half:width]
    by_tap = dot_nt(stack, oh_ref[...])
    by_tap = by_tap[6:7] + by_tap[7:8] + by_tap[8:9]
    for k in range(taps):
        ext_ref[6 + k : 7 + k, 0:vocab] = by_tap[:, k * vocab : (k + 1) * vocab]
    spot = lax.broadcasted_iota(jnp.int32, (1, half), 1)
    misc = jnp.zeros((1, half), F32)
    sums = [calibs[i][b][c] for i in range(2) for b in range(sizes) for c in range(sizes)]
    sums.append(jnp.sum(entropy, axis=1, keepdims=True))
    sums.append(jnp.sum(own * mask, axis=1, keepdims=True))
    sums.append(jnp.sum(own * gammas[1], axis=1, keepdims=True))
    for i, one in enumerate(sums):
        misc = jnp.where(spot == i, one, misc)
    ext_ref[11:12] = misc
    send_ref[span : span + 16] = coded(ext_ref[...])
    send_ref[span + 16 : span + 32] = jnp.concatenate([idt, jnp.zeros((16, half - idt.shape[1]), BF)], axis=1)


def coded(ext):
    hi = ext.astype(BF).astype(F32)
    row = lax.broadcasted_iota(jnp.int32, ext.shape, 0)
    return jnp.where(row == 12, ext[11:12] - hi[11:12], hi).astype(BF)


def decoded(code):
    wide = code.astype(F32)
    row = lax.broadcasted_iota(jnp.int32, wide.shape, 0)
    return wide + jnp.where(row == 11, wide[12:13], 0.0)


def joined(ext_ref):
    return decoded(coded(ext_ref[...]))


def pair(ref, at):
    return decoded(ref[at : at + 16])


def local_value(shape_, dim, a_mine, b_mine, vocab):
    slot = lax.broadcasted_iota(jnp.int32, shape_, dim)
    return jnp.bitwise_xor(slot, jnp.where(slot < vocab // 2, a_mine, b_mine))


def table_kernel(keep_ref, idt_ref, got_ref, ext_ref, a_keep, a_send, b_keep, b_send, ext_out, *, seq_size, part):
    span, half = keep_ref.shape
    taps, quarter, _ = a_keep.shape
    vocab = 4 * quarter
    _, a_mine, b_mine = place(seq_size, quarter, part)
    value = local_value((vocab, 1), 0, a_mine, b_mine, vocab).astype(F32)
    mine = idt_ref[...].astype(F32)
    theirs = got_ref[span + 16 : span + 32].astype(F32)
    wide = mine.shape[1]
    for k in range(taps):
        acc = None
        for i in range(span // wide):
            for ids, grad in ((mine, keep_ref), (theirs, got_ref)):
                row = ids[2 * k + i : 2 * k + i + 1, 0:wide]
                one_hot = jnp.where(row == value, 1.0, 0.0).astype(BF)
                term = dot_nn(one_hot, grad[i * wide : (i + 1) * wide])
                acc = term if acc is None else acc + term
        a_keep[k] = acc[0:quarter]
        a_send[k * quarter : (k + 1) * quarter] = acc[quarter : 2 * quarter].astype(BF)
        b_keep[k] = acc[2 * quarter : 3 * quarter]
        b_send[k * quarter : (k + 1) * quarter] = acc[3 * quarter : 4 * quarter].astype(BF)
    ext = joined(ext_ref) + pair(got_ref, span)
    ext_out[...] = ext
    a_send[taps * quarter : taps * quarter + 16] = coded(ext)


def second_kernel(a_in, b_in, a_got, b_got, ext_ref, a_keep, a_send, b_keep, b_send, ext_out):
    taps, rows, _ = a_in.shape
    part = rows // 2
    for src, got, keep, send in ((a_in, a_got, a_keep, a_send), (b_in, b_got, b_keep, b_send)):
        for k in range(taps):
            total = src[k] + got[k * rows : (k + 1) * rows].astype(F32)
            keep[k] = total[0:part]
            send[k * part : (k + 1) * part] = total[part:rows].astype(BF)
    ext = joined(ext_ref) + pair(a_got, taps * rows)
    ext_out[...] = ext
    a_send[taps * part : taps * part + 16] = coded(ext)


def third_kernel(a_in, b_in, a_got, b_got, ext_ref, keep, ext_out, *sends):
    taps, rows, _ = a_in.shape
    peers = len(sends)
    part = rows // (peers + 1)
    ext = joined(ext_ref) + pair(a_got, taps * rows)
    ext_out[...] = ext
    groups = 2 * taps
    pieces = [[] for _ in range(peers + 1)]
    for src, got in ((a_in, a_got), (b_in, b_got)):
        for k in range(taps):
            total = src[k] + got[k * rows : (k + 1) * rows].astype(F32)
            for t in range(peers + 1):
                pieces[t].append(total[t * part : (t + 1) * part])
    for t in range(peers + 1):
        block = jnp.concatenate(pieces[t], axis=0)
        if t == 0:
            keep[...] = block
        else:
            send = sends[t - 1]
            send[0 : groups * part] = block.astype(BF)
            send[groups * part : groups * part + 16] = coded(ext)


def tree_sum(items):
    while len(items) > 1:
        items = [items[i] + items[i + 1] for i in range(0, len(items), 2)]
    return items[0]


def shard_kernel(keep, ext_ref, scorer_ref, *refs, seq_size, taps, vocab):
    gots, (shard, loss_ref, bias_ref, grad_scorer_ref, calib_ref) = refs[:-5], refs[-5:]
    size, half = keep.shape
    part = size // (2 * taps)
    upper, a_mine, b_mine = place(seq_size, vocab // 4, part)
    ext = tree_sum([joined(ext_ref)] + [pair(g, size) for g in gots])
    total = tree_sum([keep[...]] + [g[0:size].astype(F32) for g in gots])
    spot = lax.broadcasted_iota(jnp.int32, (1, half), 1)
    misc = ext[11:12]

    def one(i):
        return jnp.sum(jnp.where(spot == i, misc, 0.0), axis=1, keepdims=True)

    count = one(33)
    scorer = scorer_ref[...].reshape(1, 2 * half)
    mine = jnp.where(upper, scorer[:, half:], scorer[:, :half])
    step = lax.broadcasted_iota(jnp.int32, (part, vocab), 0)
    lane = lax.broadcasted_iota(jnp.int32, (part, vocab), 1)
    pieces = []
    for g in range(2):
        hit = lane == step + (a_mine if g == 0 else vocab // 2 + b_mine)
        for k in range(taps):
            column = jnp.sum(jnp.where(hit, ext[6 + k : 7 + k, 0:vocab], 0.0), axis=1, keepdims=True)
            at = (g * taps + k) * part
            pieces.append(total[at : at + part] - (column / count) * mine)
    shard[...] = jnp.concatenate(pieces, axis=0).astype(BF)

    def whole(i):
        return jnp.concatenate([ext[i : i + 1], ext[i + 1 : i + 2]], axis=1)

    grad_scorer_ref[...] = (whole(0) - whole(2) / count).reshape(2 * half)
    bias_ref[...] = (whole(4) - (one(34) / count) * scorer).reshape(2 * half)
    row = lax.broadcasted_iota(jnp.int32, calib_ref.shape, 0)
    col = lax.broadcasted_iota(jnp.int32, calib_ref.shape, 1)
    out = jnp.zeros(calib_ref.shape, F32)
    for b in range(4):
        for c in range(4):
            out = jnp.where((row == b) & (col == c), one(4 * b + c) - one(16 + 4 * b + c) / count, out)
    calib_ref[...] = out
    loss_ref[...] = one(32) / count


def gather_kernel(*refs, taps):
    shards, (a_ref, b_ref) = refs[:-2], refs[-2:]
    part = shards[0].shape[0] // (2 * taps)
    wide = [s[...].astype(F32) for s in shards]
    for g, out in enumerate((a_ref, b_ref)):
        rows = [w[(g * taps + k) * part : (g * taps + k + 1) * part] for k in range(taps) for w in wide]
        out[...] = jnp.concatenate(rows, axis=0).astype(BF)


def double_kernel(a_ref, b_ref, a_got, b_got, early_ref, a_out, b_out, *, taps):
    rows = a_ref.shape[0] // taps
    for g, (src, got, out) in enumerate(((a_ref, a_got, a_out), (b_ref, b_got, b_out))):
        for k in range(taps):
            at = 2 * rows * k
            for first, ref in ((at, src), (at + rows, got)):
                piece = ref[k * rows : (k + 1) * rows]
                out[first : first + rows] = piece
                early_ref[g, first : first + rows] = piece


def order_kernel(table_ref, after_ref, out_ref, *, seq_size, part):
    del after_ref
    vocab = table_ref.shape[0]
    _, a_mine, b_mine = place(seq_size, vocab // 4, part)
    value = local_value((1, vocab), 1, a_mine, b_mine, vocab)
    natural = lax.broadcasted_iota(jnp.int32, (vocab, vocab), 0)
    out_ref[...] = dot_tn(table_ref[...], jnp.where(natural == value, 1.0, 0.0).astype(BF)).astype(BF)


def final_kernel(
    early, a_late, b_late, far_early, far_a, far_b, table_t_ref, weight_ref, conv_ref, table_ref, buffer, sem, *, seq_size, part,
):
    taps, width, _ = weight_ref.shape
    vocab = table_t_ref.shape[1]
    quarter = vocab // 4
    upper, a_mine, b_mine = place(seq_size, quarter, part)

    def rows_of(k):
        at = k * quarter
        near = [early[0, at : at + quarter], a_late[at : at + quarter], early[1, at : at + quarter], b_late[at : at + quarter]]
        far = [far_early[0, at : at + quarter], far_a[at : at + quarter], far_early[1, at : at + quarter], far_b[at : at + quarter]]
        near, far = jnp.concatenate(near, axis=0), jnp.concatenate(far, axis=0)
        return jnp.concatenate([jnp.where(upper, far, near), jnp.where(upper, near, far)], axis=1)

    rows = []
    for k in range(taps):
        rows.append(rows_of(k))
        buffer[k] = dot_nn(table_t_ref[...], rows[k])
        pltpu.make_async_copy(buffer.at[k], conv_ref.at[k], sem.at[k]).start()
    acc = dot_nt(rows[0], weight_ref[0])
    for k in range(1, taps):
        acc = acc + dot_nt(rows[k], weight_ref[k])
    for at in range(0, vocab, part):
        to = (at ^ a_mine) if at < vocab // 2 else vocab // 2 + ((at - vocab // 2) ^ b_mine)
        table_ref[pl.ds(pl.multiple_of(to, part), part)] = acc[at : at + part]
    for k in range(taps):
        pltpu.make_async_copy(buffer.at[k], conv_ref.at[k], sem.at[k]).wait()


def neighbour(shard, axis, by):
    length = lax.axis_size(axis)
    return lax.ppermute(shard, axis, [(i, i + by) for i in range(length) if 0 <= i + by < length])


def swap(shard, flip, count):
    return lax.ppermute(shard, AXES, [(i, i ^ flip) for i in range(count)])


def body(
    byte_ids, seg_ids, row_len, embed_table, conv_weight, conv_bias, scorer, calibration, cotangent
):
    row_count, span = byte_ids.shape
    vocab, width = embed_table.shape
    taps = conv_weight.shape[0]
    half = width // 2
    quarter = vocab // 4
    seq_size = lax.axis_size("seq")
    count = lax.axis_size("rows") * seq_size
    depth = count // 8
    assert row_count == 1 and vocab == 256 and taps == 5 and calibration.shape == (4, 4)
    assert seq_size % 2 == 0 and depth >= 1 and quarter // 2 % depth == 0
    part = quarter // 2 // depth
    eighth = quarter // 2
    size = 2 * taps * part
    lanes = span + 128

    to_right, to_left = pl.pallas_call(
        pack_kernel,
        out_shape=(shape((HALO, span), BF), shape((2 * HALO, width), BF)),
        grid=(1,),
        in_specs=[
            pl.BlockSpec((1, span), lambda i: (0, 0)),
            pl.BlockSpec((1, span), lambda i: (0, 0)),
            pl.BlockSpec((1, HALO, width), lambda i: (0, 0, 0)),
        ],
        out_specs=(pl.BlockSpec((HALO, span), lambda i: (0, 0)), pl.BlockSpec((2 * HALO, width), lambda i: (0, 0))),
        name="pack",
    )(byte_ids, seg_ids, cotangent)
    from_left = neighbour(to_right, "seq", 1)
    from_right = neighbour(to_left, "seq", -1)

    hi, lo, q_rows = pl.pallas_call(
        tap_kernel,
        out_shape=(shape((taps * vocab, width), BF), shape((taps * vocab, width), BF), shape((16, width), BF)),
        grid=(taps,),
        in_specs=[
            pl.BlockSpec((vocab, width), lambda k: (0, 0)),
            pl.BlockSpec((1, width, width), lambda k: (k, 0, 0)),
            pl.BlockSpec((width,), lambda k: (0,)),
        ],
        out_specs=(
            pl.BlockSpec((vocab, width), lambda k: (k, 0)),
            pl.BlockSpec((vocab, width), lambda k: (k, 0)),
            pl.BlockSpec((16, width), lambda k: (0, 0)),
        ),
        name="taps",
        compiler_params=pltpu.CompilerParams(vmem_limit_bytes=VMEM_LIMIT),
    )(embed_table, conv_weight, scorer)

    blocks, keep, send, ext, idt = call(
        functools.partial(local_kernel, seq_size=seq_size, taps=taps),
        (
            shape((1, span // 2, width), BF),
            shape((span, half), BF),
            shape((span + 32, half), BF),
            shape((16, half), F32),
            shape((16, span // 2), BF),
        ),
        "local",
        in_specs=[sspec(), sspec()] + [vspec()] * 9,
        out_specs=(vspec(),) * 5,
        scratch_shapes=[
            pltpu.VMEM((lanes, width), BF),
            pltpu.VMEM((span // 2 + 2 * HALO, width), BF),
            pltpu.VMEM((taps * vocab, lanes), BF),
        ],
    )(row_len, calibration, byte_ids, seg_ids, from_left, from_right, hi, lo, conv_bias, cotangent, q_rows)

    got = swap(send, 1, count)
    a_keep, a_send, b_keep, b_send, ext = call(
        functools.partial(table_kernel, seq_size=seq_size, part=part),
        (
            shape((taps, quarter, half), F32),
            shape((taps * quarter + 16, half), BF),
            shape((taps, quarter, half), F32),
            shape((taps * quarter, half), BF),
            shape((16, half), F32),
        ),
        "by_value",
        in_specs=[vspec()] * 4,
        out_specs=(vspec(),) * 5,
    )(keep, idt, got, ext)
    table_t = call(
        functools.partial(order_kernel, seq_size=seq_size, part=part),
        shape((width, vocab), BF),
        "order",
        in_specs=[vspec()] * 2,
        out_specs=vspec(),
    )(embed_table, ext)

    a_got, b_got = swap(a_send, 2, count), swap(b_send, 4, count)
    a_keep, a_send, b_keep, b_send, ext = call(
        second_kernel,
        (
            shape((taps, eighth, half), F32),
            shape((taps * eighth + 16, half), BF),
            shape((taps, eighth, half), F32),
            shape((taps * eighth, half), BF),
            shape((16, half), F32),
        ),
        "second",
        in_specs=[vspec()] * 5,
        out_specs=(vspec(),) * 5,
    )(a_keep, b_keep, a_got, b_got, ext)

    a_got, b_got = swap(a_send, 4, count), swap(b_send, 2, count)
    outs = call(
        third_kernel,
        (shape((size, half), F32), shape((16, half), F32)) + (shape((size + 16, half), BF),) * (depth - 1),
        "third",
        in_specs=[vspec()] * 5,
        out_specs=(vspec(),) * (depth + 1),
    )(a_keep, b_keep, a_got, b_got, ext)
    mine, ext, sends = outs[0], outs[1], outs[2:]
    gots = [swap(s, 8 * (t + 1), count) for t, s in enumerate(sends)]
    shard, loss, grad_bias, grad_scorer, grad_calib = call(
        functools.partial(shard_kernel, seq_size=seq_size, taps=taps, vocab=vocab),
        (shape((size, half), BF), shape((1, 1), F32), shape((width,), F32), shape((width,), F32), shape((4, 4), F32)),
        "shard",
        in_specs=[vspec()] * (3 + len(gots)),
        out_specs=(vspec(),) * 5,
    )(mine, ext, scorer, *gots)

    gathered = [shard] + [swap(shard, 8 * t, count) for t in range(1, depth)]
    a_out, b_out = call(
        functools.partial(gather_kernel, taps=taps),
        (shape((taps * eighth, half), BF),) * 2,
        "gather",
        in_specs=[vspec()] * depth,
        out_specs=(vspec(),) * 2,
    )(*gathered)
    a_got, b_got = swap(a_out, 4, count), swap(b_out, 2, count)
    early, a_out, b_out = call(
        functools.partial(double_kernel, taps=taps),
        (shape((2, taps * quarter, half), BF),) + (shape((taps * quarter, half), BF),) * 2,
        "double",
        in_specs=[vspec()] * 4,
        out_specs=(vspec(),) * 3,
    )(a_out, b_out, a_got, b_got)
    a_late, b_late = swap(a_out, 2, count), swap(b_out, 4, count)
    far_early = swap(early, 1, count)
    far_a, far_b = swap(a_late, 1, count), swap(b_late, 1, count)

    conv, table = call(
        functools.partial(final_kernel, seq_size=seq_size, part=part),
        (shape((taps, width, width), F32), shape((vocab, width), F32)),
        "final",
        in_specs=[vspec()] * 8,
        out_specs=(pl.BlockSpec(memory_space=pl.ANY), vspec()),
        scratch_shapes=[pltpu.VMEM((taps, width, width), F32), pltpu.SemaphoreType.DMA((taps,))],
    )(early, a_late, b_late, far_early, far_a, far_b, table_t, conv_weight)
    return (blocks, loss.reshape(()), table, conv, grad_bias, grad_scorer, grad_calib)


def solution(mesh):
    return jax.shard_map(
        body,
        mesh=mesh,
        in_specs=(
            P("rows", "seq"),
            P("rows", "seq"),
            P("rows"),
            P(),
            P(),
            P(),
            P(),
            P(),
            P("rows", "seq", None),
        ),
        out_specs=(P("rows", "seq", None), P(), P(), P(), P(), P(), P()),
        check_vma=False,
    )
```

```python
import functools

import jax
import jax.numpy as jnp
from jax import lax
from jax.experimental import pallas as pl
from jax.experimental.pallas import tpu as pltpu
from jax.sharding import PartitionSpec as P

AXES = ("rows", "seq")
BF = jnp.bfloat16
F32 = jnp.float32
HALO = 16
VMEM_LIMIT = 20 * 1024 * 1024
TAPS_LIMIT = 50331648


def dot_nn(a, b):
    return lax.dot_general(a, b, (((1,), (0,)), ((), ())), preferred_element_type=F32)


def dot_nt(a, b):
    return lax.dot_general(a, b, (((1,), (1,)), ((), ())), preferred_element_type=F32)


def dot_tn(a, b):
    return lax.dot_general(a, b, (((0,), (0,)), ((), ())), preferred_element_type=F32)


def split2(v):
    hi = v.astype(BF)
    return hi, (v - hi.astype(F32)).astype(BF)


def split3(v):
    hi = v.astype(BF)
    rest = v - hi.astype(F32)
    mid = rest.astype(BF)
    return hi, mid, (rest - mid.astype(F32)).astype(BF)


def call(kernel, outs, name, **kw):
    return pl.pallas_call(
        kernel,
        out_shape=outs,
        name=name,
        compiler_params=pltpu.CompilerParams(vmem_limit_bytes=VMEM_LIMIT),
        **kw,
    )


def vspec():
    return pl.BlockSpec(memory_space=pltpu.VMEM)


def hspec():
    return pl.BlockSpec(memory_space=pltpu.HBM)


def sspec():
    return pl.BlockSpec(memory_space=pltpu.SMEM)


def shape(dims, dtype):
    return jax.ShapeDtypeStruct(dims, dtype)


def place(seq_size, quarter, part):
    device = lax.axis_index("rows") * seq_size + lax.axis_index("seq")
    x_bit = (device >> 1) & 1
    y_bit = (device >> 2) & 1
    rest = (device >> 3) * part
    a_mine = x_bit * quarter + y_bit * (quarter // 2) + rest
    b_mine = y_bit * quarter + x_bit * (quarter // 2) + rest
    return (device & 1) == 1, a_mine, b_mine


def pack_kernel(row_len_ref, ids_ref, seg_ref, cot_ref, scorer_ref, right_ref, left_ref, q_ref):
    span = ids_ref.shape[1]
    width = cot_ref.shape[2]
    row = lax.broadcasted_iota(jnp.int32, (HALO, span), 0)
    ids = ids_ref[...].astype(F32)
    segs = seg_ref[...].astype(F32)
    length = row_len_ref[...]
    both = jnp.where(row == 0, ids, jnp.where(row == 1, segs, 0.0))
    size = jnp.where(row == 2, lax.shift_right_logical(length, 8), length & 255).astype(F32)
    both = jnp.where((row == 2) | (row == 3), size, both).astype(BF)
    right_ref[...] = both
    left_ref[0:HALO] = cot_ref[0]
    left_ref[HALO : 2 * HALO, 0:span] = both
    left_ref[HALO : 2 * HALO, span:width] = jnp.zeros((HALO, width - span), BF)
    s1, s2, s3 = split3(scorer_ref[...].reshape(1, width))
    row = lax.broadcasted_iota(jnp.int32, q_ref.shape, 0)
    pick = jnp.where(row == 0, s1.astype(F32), jnp.where(row == 1, s2.astype(F32), s3.astype(F32)))
    q_ref[...] = jnp.where(row < 3, pick, 0.0).astype(BF)


def tap_kernel(table_hbm, weight_hbm, hi_ref, lo_ref, table_ref, weight_ref, sem):
    taps = weight_ref.shape[0]
    vocab = table_ref.shape[0]
    copies = [pltpu.make_async_copy(weight_hbm.at[k], weight_ref.at[k], sem.at[k]) for k in range(taps)]
    copies.insert(0, pltpu.make_async_copy(table_hbm, table_ref, sem.at[taps]))
    for copy in copies:
        copy.start()
    copies[0].wait()
    for k in range(taps):
        copies[1 + k].wait()
        hi, lo = split2(dot_nn(table_ref[...], weight_ref[k]))
        hi_ref[k * vocab : (k + 1) * vocab] = hi
        lo_ref[k * vocab : (k + 1) * vocab] = lo


def roll(v, by):
    by = by % v.shape[1]
    return pltpu.roll(v, by, 1) if by else v


def local_kernel(
    calib_ref, mine_ref, from_left_ref, from_right_ref, hi_ref, lo_ref, bias_ref, cot_ref,
    q_ref, keep_ref, send_ref, ext_ref, idt_ref, band_ref, y_ref, full_q_ref, *, seq_size, taps,
):
    span = keep_ref.shape[0]
    width = hi_ref.shape[1]
    vocab = hi_ref.shape[0] // taps
    half = width // 2
    own_blocks = span // 2
    lanes = y_ref.shape[0]
    sizes = calib_ref.shape[0]
    front = span + HALO
    upper = place(seq_size, 1, 1)[0]
    spare = lax.broadcasted_iota(jnp.int32, (1, lanes - span), 1)

    mine = mine_ref[...].astype(F32)
    length = (256.0 * mine[2:3, 0:1] + mine[3:4, 0:1]).astype(jnp.int32)

    def line_up(at):
        near_right = from_right_ref[HALO : 2 * HALO, 0 : lanes - span].astype(F32)[at : at + 1]
        near_left = from_left_ref[:, 2 * span - lanes : span].astype(F32)[at : at + 1]
        rest = jnp.where(spare < HALO, near_right, jnp.where(spare >= lanes - span - HALO, near_left, 0.0))
        return jnp.concatenate([mine[at : at + 1], rest], axis=1)

    pos = lax.broadcasted_iota(jnp.int32, (1, lanes), 1)
    own = jnp.where(pos < span, 1.0, 0.0)
    place_in_row = lax.axis_index("seq") * span + jnp.where(pos < front, pos, pos - lanes)
    near = (pos < front) | (pos >= lanes - HALO)
    mask = jnp.where(near & (place_in_row >= 0) & (place_in_row < length), 1.0, 0.0)
    seg = line_up(1)
    known = jnp.where(mask > 0.5, line_up(0), -1.0)
    row16 = lax.broadcasted_iota(jnp.int32, (16, span // 2), 0)
    row8 = lax.broadcasted_iota(jnp.int32, (8, lanes), 0)
    idt = jnp.zeros((16, span // 2), F32)
    by_tap = jnp.zeros((8, lanes), F32)
    for k in range(taps):
        moved = roll(known, taps - 1 - k)
        by_tap = jnp.where(row8 == k, moved, by_tap)
        for i in range(2):
            idt = jnp.where(row16 == 2 * k + i, moved[:, i * (span // 2) : (i + 1) * (span // 2)], idt)
    idt = idt.astype(BF)
    idt_ref[...] = idt
    column = jnp.transpose(by_tap)
    column = jnp.concatenate([column[0:front], column[lanes - HALO : lanes]], axis=0)
    value = lax.broadcasted_iota(jnp.int32, (front + HALO, vocab), 1).astype(F32)
    one_hot = [jnp.where(column[:, k : k + 1] == value, 1.0, 0.0).astype(BF) for k in range(taps)]
    one_hot = jnp.concatenate(one_hot, axis=1)
    y = dot_nn(one_hot, hi_ref[...]) + dot_nn(one_hot, lo_ref[...])
    y = (y + bias_ref[...].reshape(1, width)).astype(BF)
    y_ref[0:front] = y[0:front]
    y_ref[front : lanes - HALO] = jnp.zeros((lanes - HALO - front, width), BF)
    y_ref[lanes - HALO : lanes] = y[front : front + HALO]
    full_q_ref[0:own_blocks] = cot_ref[0]
    full_q_ref[own_blocks : own_blocks + HALO] = from_right_ref[0:HALO]
    full_q_ref[own_blocks + HALO : own_blocks + 2 * HALO] = q_ref[...]
    tail = own_blocks + HALO
    q_rows = own_blocks + 2 * HALO
    dots = dot_nt(full_q_ref[...], y_ref[...])
    u = dots[tail : tail + 1] + dots[tail + 1 : tail + 2] + dots[tail + 2 : tail + 3]

    line = lax.broadcasted_iota(jnp.int32, (q_rows, lanes), 0)
    valid, match, grads = [], [], []
    for d in range(sizes):
        valid.append(mask * roll(mask, d) * jnp.where(seg == roll(seg, d), 1.0, 0.0))
        ahead = jnp.where(pos + d >= lanes, pos + d - lanes, pos + d)
        block = jnp.where(ahead < front, lax.shift_right_logical(ahead, 1), -1)
        match.append(line == block)
        picked = jnp.sum(jnp.where(match[d], dots, 0.0), axis=0, keepdims=True)
        grads.append(0.5 * roll(picked, d))
    counted, inv, scores, dprobs = 0.0, [], [], []
    run_u, run_g = 0.0, 0.0
    for d in range(sizes):
        counted = counted + valid[d]
        inv.append(1.0 / jnp.maximum(counted, 1.0))
        run_u = run_u + valid[d] * roll(u, d)
        run_g = run_g + valid[d] * grads[d]
        scores.append(run_u * inv[d])
        dprobs.append(run_g * inv[d])
    logits = [sum(scores[b] * calib_ref[b, c] for b in range(sizes)) for c in range(sizes)]
    top = logits[0]
    for c in range(1, sizes):
        top = jnp.maximum(top, logits[c])
    powers = [jnp.exp(v - top) for v in logits]
    total = sum(powers)
    probs = [v / total for v in powers]
    lse = top + jnp.log(total)
    mean_logit = sum(p * v for p, v in zip(probs, logits))
    mean_grad = sum(p * v for p, v in zip(probs, dprobs))
    entropy = own * mask * (lse - mean_logit)
    parts = [
        [p * (v - mean_grad) for p, v in zip(probs, dprobs)],
        [mask * p * (v - mean_logit) for p, v in zip(probs, logits)],
    ]
    alpha, later = [None] * sizes, 0.0
    for d in reversed(range(sizes)):
        later = later + probs[d] * inv[d]
        alpha[d] = valid[d] * later
    gammas, rhos, calibs = [], [], []
    for part in parts:
        dscores = [sum(part[c] * calib_ref[b, c] for c in range(sizes)) for b in range(sizes)]
        later, gamma, rho = 0.0, 0.0, 0.0
        for d in reversed(range(sizes)):
            later = later + inv[d] * dscores[d]
            beta = valid[d] * later
            gamma = gamma + roll(beta, -d)
            rho = rho + roll(beta * own, -d)
        gammas.append(gamma)
        rhos.append(rho)
        calibs.append([[jnp.sum(own * scores[b] * part[c], axis=1, keepdims=True) for c in range(sizes)] for b in range(sizes)])
    band = jnp.where((line >= tail) & (line < tail + 3), gammas[0], 0.0)
    for d in range(sizes):
        band = band + jnp.where(match[d], 0.5 * roll(alpha[d], -d), 0.0)
    band_hi, band_lo = split2(band)
    band_ref[0] = band_hi[0:own_blocks]
    band_ref[1] = band_lo[0:own_blocks]
    dy = dot_tn(band_hi[:, 0:span], full_q_ref[...]) + dot_tn(band_lo[:, 0:span], full_q_ref[...])
    dy = dy.astype(BF)
    left, right = dy[:, 0:half], dy[:, half:width]
    keep_ref[...] = jnp.where(upper, right, left)
    send_ref[0:span] = jnp.where(upper, left, right)
    grad_bias = jnp.sum(dy.astype(F32), axis=0, keepdims=True)

    row16 = lax.broadcasted_iota(jnp.int32, (16, lanes), 0)
    stack = jnp.zeros((16, lanes), F32)
    pieces = split3(rhos[0]) + split3(rhos[1]) + split3(gammas[1] * own)
    for i, piece in enumerate(pieces):
        stack = jnp.where(row16 == i, piece.astype(F32), stack)
    stack = stack.astype(BF)
    by_y = dot_nn(stack, y_ref[...])
    grad_scorer = [by_y[3 * i : 3 * i + 1] + by_y[3 * i + 1 : 3 * i + 2] + by_y[3 * i + 2 : 3 * i + 3] for i in range(2)]
    ext_ref[...] = jnp.zeros(ext_ref.shape, F32)
    for i, row in enumerate(grad_scorer + [grad_bias]):
        ext_ref[2 * i : 2 * i + 1] = row[:, 0:half]
        ext_ref[2 * i + 1 : 2 * i + 2] = row[:, half:width]
    by_tap = dot_nn(stack[:, 0:span], one_hot[0:span])
    by_tap = by_tap[6:7] + by_tap[7:8] + by_tap[8:9]
    by_tap = jnp.concatenate([by_tap, jnp.zeros((1, 4 * half - taps * vocab), F32)], axis=1)
    for i in range(4):
        ext_ref[6 + i : 7 + i] = by_tap[:, i * half : (i + 1) * half]
    spot = lax.broadcasted_iota(jnp.int32, (1, half), 1)
    misc = jnp.zeros((1, half), F32)
    sums = [calibs[i][b][c] for i in range(2) for b in range(sizes) for c in range(sizes)]
    sums.append(jnp.sum(entropy, axis=1, keepdims=True))
    sums.append(jnp.sum(own * mask, axis=1, keepdims=True))
    sums.append(jnp.sum(own * gammas[1], axis=1, keepdims=True))
    for i, one in enumerate(sums):
        misc = jnp.where(spot == i, one, misc)
    ext_ref[10:11] = misc
    send_ref[span : span + 16] = coded(ext_ref[...])
    send_ref[span + 16 : span + 32] = jnp.concatenate([idt, jnp.zeros((16, half - idt.shape[1]), BF)], axis=1)


def mix_kernel(band_ref, y_ref, blocks_ref, token_ref):
    blocks_ref[0] = (dot_nn(band_ref[0], y_ref[...]) + dot_nn(band_ref[1], y_ref[...])).astype(BF)
    token_ref[...] = jnp.zeros(token_ref.shape, F32)


def coded(ext):
    hi = ext.astype(BF).astype(F32)
    lo = ext - hi
    return jnp.concatenate([hi[0:11], lo[0:2], lo[4:6], lo[10:11]], axis=0).astype(BF)


def decoded(code):
    w = code.astype(F32)
    rows = [w[0:2] + w[11:13], w[2:4], w[4:6] + w[13:15], w[6:10], w[10:11] + w[15:16], jnp.zeros((5, w.shape[1]), F32)]
    return jnp.concatenate(rows, axis=0)


def joined(ext_ref):
    return decoded(coded(ext_ref[...]))


def pair(ref, at):
    return decoded(ref[at : at + 16])


def local_value(shape_, dim, a_mine, b_mine, vocab):
    slot = lax.broadcasted_iota(jnp.int32, shape_, dim)
    return jnp.bitwise_xor(slot, jnp.where(slot < vocab // 2, a_mine, b_mine))


def table_kernel(keep_ref, idt_ref, got_ref, ext_ref, a_keep, a_send, b_keep, b_send, ext_out, *, seq_size, part):
    span, half = keep_ref.shape
    taps, quarter, _ = a_keep.shape
    vocab = 4 * quarter
    _, a_mine, b_mine = place(seq_size, quarter, part)
    value = local_value((vocab, 1), 0, a_mine, b_mine, vocab).astype(F32)
    mine = idt_ref[...].astype(F32)
    theirs = got_ref[span + 16 : span + 32].astype(F32)
    wide = mine.shape[1]
    for k in range(taps):
        acc = None
        for i in range(span // wide):
            for ids, grad in ((mine, keep_ref), (theirs, got_ref)):
                row = ids[2 * k + i : 2 * k + i + 1, 0:wide]
                one_hot = jnp.where(row == value, 1.0, 0.0).astype(BF)
                term = dot_nn(one_hot, grad[i * wide : (i + 1) * wide])
                acc = term if acc is None else acc + term
        a_keep[k] = acc[0:quarter]
        a_send[k * quarter : (k + 1) * quarter] = acc[quarter : 2 * quarter].astype(BF)
        b_keep[k] = acc[2 * quarter : 3 * quarter]
        b_send[k * quarter : (k + 1) * quarter] = acc[3 * quarter : 4 * quarter].astype(BF)
    ext = joined(ext_ref) + pair(got_ref, span)
    ext_out[...] = ext
    a_send[taps * quarter : taps * quarter + 16] = coded(ext)


def second_kernel(a_in, b_in, a_got, b_got, ext_ref, mixed_ref, order_ref, a_keep, a_send, b_keep, b_send, ext_out):
    del mixed_ref, order_ref
    taps, rows, _ = a_in.shape
    part = rows // 2
    for src, got, keep, send in ((a_in, a_got, a_keep, a_send), (b_in, b_got, b_keep, b_send)):
        for k in range(taps):
            total = src[k] + got[k * rows : (k + 1) * rows].astype(F32)
            keep[k] = total[0:part]
            send[k * part : (k + 1) * part] = total[part:rows].astype(BF)
    ext = joined(ext_ref) + pair(a_got, taps * rows)
    ext_out[...] = ext
    a_send[taps * part : taps * part + 16] = coded(ext)


def third_kernel(a_in, b_in, a_got, b_got, ext_ref, keep, ext_out, *sends):
    taps, rows, _ = a_in.shape
    peers = len(sends)
    part = rows // (peers + 1)
    ext = joined(ext_ref) + pair(a_got, taps * rows)
    ext_out[...] = ext
    groups = 2 * taps
    pieces = [[] for _ in range(peers + 1)]
    for src, got in ((a_in, a_got), (b_in, b_got)):
        for k in range(taps):
            total = src[k] + got[k * rows : (k + 1) * rows].astype(F32)
            for t in range(peers + 1):
                pieces[t].append(total[t * part : (t + 1) * part])
    for t in range(peers + 1):
        block = jnp.concatenate(pieces[t], axis=0)
        if t == 0:
            keep[...] = block
        else:
            send = sends[t - 1]
            send[0 : groups * part] = block.astype(BF)
            send[groups * part : groups * part + 16] = coded(ext)


def tree_sum(items):
    while len(items) > 1:
        items = [items[i] + items[i + 1] for i in range(0, len(items), 2)]
    return items[0]


def shard_kernel(keep, ext_ref, scorer_ref, *refs, seq_size, taps, vocab):
    gots, (shard, loss_ref, bias_ref, grad_scorer_ref, calib_ref) = refs[:-5], refs[-5:]
    size, half = keep.shape
    part = size // (2 * taps)
    upper, a_mine, b_mine = place(seq_size, vocab // 4, part)
    ext = tree_sum([joined(ext_ref)] + [pair(g, size) for g in gots])
    total = tree_sum([keep[...]] + [g[0:size].astype(F32) for g in gots])
    spot = lax.broadcasted_iota(jnp.int32, (1, half), 1)
    misc = ext[10:11]
    by_tap = jnp.concatenate([ext[i : i + 1] for i in range(6, 10)], axis=1)

    def one(i):
        return jnp.sum(jnp.where(spot == i, misc, 0.0), axis=1, keepdims=True)

    count = one(33)
    scorer = scorer_ref[...].astype(F32)
    scorer = scorer[0:1] + scorer[1:2] + scorer[2:3]
    mine = jnp.where(upper, scorer[:, half:], scorer[:, :half])
    step = lax.broadcasted_iota(jnp.int32, (part, vocab), 0)
    lane = lax.broadcasted_iota(jnp.int32, (part, vocab), 1)
    pieces = []
    for g in range(2):
        hit = lane == step + (a_mine if g == 0 else vocab // 2 + b_mine)
        for k in range(taps):
            column = jnp.sum(jnp.where(hit, by_tap[:, k * vocab : (k + 1) * vocab], 0.0), axis=1, keepdims=True)
            at = (g * taps + k) * part
            pieces.append(total[at : at + part] - (column / count) * mine)
    shard[...] = jnp.concatenate(pieces, axis=0).astype(BF)

    def whole(i):
        return jnp.concatenate([ext[i : i + 1], ext[i + 1 : i + 2]], axis=1)

    grad_scorer_ref[...] = (whole(0) - whole(2) / count).reshape(2 * half)
    bias_ref[...] = (whole(4) - (one(34) / count) * scorer).reshape(2 * half)
    row = lax.broadcasted_iota(jnp.int32, calib_ref.shape, 0)
    col = lax.broadcasted_iota(jnp.int32, calib_ref.shape, 1)
    out = jnp.zeros(calib_ref.shape, F32)
    for b in range(4):
        for c in range(4):
            out = jnp.where((row == b) & (col == c), one(4 * b + c) - one(16 + 4 * b + c) / count, out)
    calib_ref[...] = out
    loss_ref[...] = one(32) / count


def gather_kernel(*refs, taps):
    shards, (a_ref, b_ref) = refs[:-2], refs[-2:]
    part = shards[0].shape[0] // (2 * taps)
    wide = [s[...].astype(F32) for s in shards]
    for g, out in enumerate((a_ref, b_ref)):
        rows = [w[(g * taps + k) * part : (g * taps + k + 1) * part] for k in range(taps) for w in wide]
        out[...] = jnp.concatenate(rows, axis=0).astype(BF)


def double_kernel(a_ref, b_ref, a_got, b_got, early_ref, a_out, b_out, *, taps):
    rows = a_ref.shape[0] // taps
    for g, (src, got, out) in enumerate(((a_ref, a_got, a_out), (b_ref, b_got, b_out))):
        for k in range(taps):
            at = 2 * rows * k
            for first, ref in ((at, src), (at + rows, got)):
                piece = ref[k * rows : (k + 1) * rows]
                out[first : first + rows] = piece
                early_ref[g, first : first + rows] = piece


def order_kernel(table_ref, after_ref, out_ref, token_ref, *, seq_size, part):
    del after_ref
    token_ref[...] = jnp.zeros(token_ref.shape, F32)
    vocab = table_ref.shape[0]
    _, a_mine, b_mine = place(seq_size, vocab // 4, part)
    value = local_value((1, vocab), 1, a_mine, b_mine, vocab)
    natural = lax.broadcasted_iota(jnp.int32, (vocab, vocab), 0)
    out_ref[...] = dot_tn(table_ref[...], jnp.where(natural == value, 1.0, 0.0).astype(BF)).astype(BF)


def final_kernel(
    early, a_late, b_late, far_early, far_a, far_b, table_t_ref, weight_ref, conv_ref, table_ref, buffer, sem, *, seq_size, part,
):
    taps, width, _ = weight_ref.shape
    vocab = table_t_ref.shape[1]
    quarter = vocab // 4
    upper, a_mine, b_mine = place(seq_size, quarter, part)

    def rows_of(k):
        at = k * quarter
        near = [early[0, at : at + quarter], a_late[at : at + quarter], early[1, at : at + quarter], b_late[at : at + quarter]]
        far = [far_early[0, at : at + quarter], far_a[at : at + quarter], far_early[1, at : at + quarter], far_b[at : at + quarter]]
        near, far = jnp.concatenate(near, axis=0), jnp.concatenate(far, axis=0)
        return jnp.concatenate([jnp.where(upper, far, near), jnp.where(upper, near, far)], axis=1)

    rows = []
    for k in range(taps):
        rows.append(rows_of(k))
        buffer[k] = dot_nn(table_t_ref[...], rows[k])
        pltpu.make_async_copy(buffer.at[k], conv_ref.at[k], sem.at[k]).start()
    acc = 0.0
    for k in range(taps):
        acc = acc + dot_nt(rows[k], weight_ref[k])
    for at in range(0, vocab, part):
        to = (at ^ a_mine) if at < vocab // 2 else vocab // 2 + ((at - vocab // 2) ^ b_mine)
        table_ref[pl.ds(pl.multiple_of(to, part), part)] = acc[at : at + part]
    for k in range(taps):
        pltpu.make_async_copy(buffer.at[k], conv_ref.at[k], sem.at[k]).wait()


def neighbour(shard, axis, by):
    length = lax.axis_size(axis)
    return lax.ppermute(shard, axis, [(i, i + by) for i in range(length) if 0 <= i + by < length])


def swap(shard, flip, count):
    return lax.ppermute(shard, AXES, [(i, i ^ flip) for i in range(count)])


def body(
    byte_ids, seg_ids, row_len, embed_table, conv_weight, conv_bias, scorer, calibration, cotangent
):
    row_count, span = byte_ids.shape
    vocab, width = embed_table.shape
    taps = conv_weight.shape[0]
    half = width // 2
    quarter = vocab // 4
    seq_size = lax.axis_size("seq")
    count = lax.axis_size("rows") * seq_size
    depth = count // 8
    assert row_count == 1 and vocab == 256 and taps == 5 and calibration.shape == (4, 4)
    assert seq_size % 2 == 0 and depth >= 1 and quarter // 2 % depth == 0
    part = quarter // 2 // depth
    eighth = quarter // 2
    size = 2 * taps * part
    lanes = span + 128

    to_right, to_left, q_rows = pl.pallas_call(
        pack_kernel,
        out_shape=(shape((HALO, span), BF), shape((2 * HALO, width), BF), shape((16, width), BF)),
        grid=(1,),
        in_specs=[
            pl.BlockSpec((1, 1), lambda i: (0, 0)),
            pl.BlockSpec((1, span), lambda i: (0, 0)),
            pl.BlockSpec((1, span), lambda i: (0, 0)),
            pl.BlockSpec((1, HALO, width), lambda i: (0, 0, 0)),
            pl.BlockSpec((width,), lambda i: (0,)),
        ],
        out_specs=(
            pl.BlockSpec((HALO, span), lambda i: (0, 0)),
            pl.BlockSpec((2 * HALO, width), lambda i: (0, 0)),
            pl.BlockSpec((16, width), lambda i: (0, 0)),
        ),
        name="pack",
    )(row_len.reshape(1, 1), byte_ids, seg_ids, cotangent, scorer)
    from_left = neighbour(to_right, "seq", 1)
    from_right = neighbour(to_left, "seq", -1)

    hi, lo = pl.pallas_call(
        tap_kernel,
        out_shape=(shape((taps * vocab, width), BF),) * 2,
        name="taps",
        in_specs=[hspec()] * 2,
        out_specs=(vspec(),) * 2,
        scratch_shapes=[
            pltpu.VMEM((vocab, width), BF),
            pltpu.VMEM((taps, width, width), BF),
            pltpu.SemaphoreType.DMA((taps + 1,)),
        ],
        compiler_params=pltpu.CompilerParams(vmem_limit_bytes=TAPS_LIMIT),
    )(embed_table, conv_weight)

    keep, send, ext, idt, band, y = call(
        functools.partial(local_kernel, seq_size=seq_size, taps=taps),
        (
            shape((span, half), BF),
            shape((span + 32, half), BF),
            shape((16, half), F32),
            shape((16, span // 2), BF),
            shape((2, span // 2, lanes), BF),
            shape((lanes, width), BF),
        ),
        "local",
        in_specs=[sspec()] + [vspec()] * 8,
        out_specs=(vspec(),) * 6,
        scratch_shapes=[pltpu.VMEM((span // 2 + 2 * HALO, width), BF)],
    )(calibration, to_right, from_left, from_right, hi, lo, conv_bias, cotangent, q_rows)

    got = swap(send, 1, count)
    a_keep, a_send, b_keep, b_send, ext = call(
        functools.partial(table_kernel, seq_size=seq_size, part=part),
        (
            shape((taps, quarter, half), F32),
            shape((taps * quarter + 16, half), BF),
            shape((taps, quarter, half), F32),
            shape((taps * quarter, half), BF),
            shape((16, half), F32),
        ),
        "by_value",
        in_specs=[vspec()] * 4,
        out_specs=(vspec(),) * 5,
    )(keep, idt, got, ext)
    token = shape((8, 128), F32)
    blocks, mixed = call(
        mix_kernel,
        (shape((1, span // 2, width), BF), token),
        "mix",
        in_specs=[vspec()] * 2,
        out_specs=(vspec(),) * 2,
    )(band, y)
    table_t, ordered = call(
        functools.partial(order_kernel, seq_size=seq_size, part=part),
        (shape((width, vocab), BF), token),
        "order",
        in_specs=[vspec()] * 2,
        out_specs=(vspec(),) * 2,
    )(embed_table, ext)

    a_got, b_got = swap(a_send, 2, count), swap(b_send, 4, count)
    a_keep, a_send, b_keep, b_send, ext = call(
        second_kernel,
        (
            shape((taps, eighth, half), F32),
            shape((taps * eighth + 16, half), BF),
            shape((taps, eighth, half), F32),
            shape((taps * eighth, half), BF),
            shape((16, half), F32),
        ),
        "second",
        in_specs=[vspec()] * 7,
        out_specs=(vspec(),) * 5,
    )(a_keep, b_keep, a_got, b_got, ext, mixed, ordered)

    a_got, b_got = swap(a_send, 4, count), swap(b_send, 2, count)
    outs = call(
        third_kernel,
        (shape((size, half), F32), shape((16, half), F32)) + (shape((size + 16, half), BF),) * (depth - 1),
        "third",
        in_specs=[vspec()] * 5,
        out_specs=(vspec(),) * (depth + 1),
    )(a_keep, b_keep, a_got, b_got, ext)
    mine, ext, sends = outs[0], outs[1], outs[2:]
    gots = [swap(s, 8 * (t + 1), count) for t, s in enumerate(sends)]
    shard, loss, grad_bias, grad_scorer, grad_calib = call(
        functools.partial(shard_kernel, seq_size=seq_size, taps=taps, vocab=vocab),
        (shape((size, half), BF), shape((1, 1), F32), shape((width,), F32), shape((width,), F32), shape((4, 4), F32)),
        "shard",
        in_specs=[vspec()] * (3 + len(gots)),
        out_specs=(vspec(),) * 5,
    )(mine, ext, q_rows, *gots)

    gathered = [shard] + [swap(shard, 8 * t, count) for t in range(1, depth)]
    a_out, b_out = call(
        functools.partial(gather_kernel, taps=taps),
        (shape((taps * eighth, half), BF),) * 2,
        "gather",
        in_specs=[vspec()] * depth,
        out_specs=(vspec(),) * 2,
    )(*gathered)
    a_got, b_got = swap(a_out, 4, count), swap(b_out, 2, count)
    early, a_out, b_out = call(
        functools.partial(double_kernel, taps=taps),
        (shape((2, taps * quarter, half), BF),) + (shape((taps * quarter, half), BF),) * 2,
        "double",
        in_specs=[vspec()] * 4,
        out_specs=(vspec(),) * 3,
    )(a_out, b_out, a_got, b_got)
    a_late, b_late = swap(a_out, 2, count), swap(b_out, 4, count)
    far_early = swap(early, 1, count)
    far_a, far_b = swap(a_late, 1, count), swap(b_late, 1, count)

    conv, grad_table = call(
        functools.partial(final_kernel, seq_size=seq_size, part=part),
        (shape((taps, width, width), F32), shape((vocab, width), F32)),
        "final",
        in_specs=[vspec()] * 8,
        out_specs=(hspec(), vspec()),
        scratch_shapes=[
            pltpu.VMEM((taps, width, width), F32),
            pltpu.SemaphoreType.DMA((taps,)),
        ],
    )(early, a_late, b_late, far_early, far_a, far_b, table_t, conv_weight)
    return (blocks, loss.reshape(()), grad_table, conv, grad_bias, grad_scorer, grad_calib)


def solution(mesh):
    return jax.shard_map(
        body,
        mesh=mesh,
        in_specs=(
            P("rows", "seq"),
            P("rows", "seq"),
            P("rows"),
            P(),
            P(),
            P(),
            P(),
            P(),
            P("rows", "seq", None),
        ),
        out_specs=(P("rows", "seq", None), P(), P(), P(), P(), P(), P()),
        check_vma=False,
    )
```

```python
import functools

import jax
import jax.numpy as jnp
from jax import lax
from jax.experimental import pallas as pl
from jax.experimental.pallas import tpu as pltpu
from jax.sharding import PartitionSpec as P

AXES = ("rows", "seq")
BF = jnp.bfloat16
F32 = jnp.float32
HALO = 16
VMEM_LIMIT = 20 * 1024 * 1024
TAPS_LIMIT = 50331648


def dot_nn(a, b):
    return lax.dot_general(a, b, (((1,), (0,)), ((), ())), preferred_element_type=F32)


def dot_nt(a, b):
    return lax.dot_general(a, b, (((1,), (1,)), ((), ())), preferred_element_type=F32)


def dot_tn(a, b):
    return lax.dot_general(a, b, (((0,), (0,)), ((), ())), preferred_element_type=F32)


def split2(v):
    hi = v.astype(BF)
    return hi, (v - hi.astype(F32)).astype(BF)


def split3(v):
    hi = v.astype(BF)
    rest = v - hi.astype(F32)
    mid = rest.astype(BF)
    return hi, mid, (rest - mid.astype(F32)).astype(BF)


def call(kernel, outs, name, **kw):
    return pl.pallas_call(
        kernel,
        out_shape=outs,
        name=name,
        compiler_params=pltpu.CompilerParams(vmem_limit_bytes=VMEM_LIMIT),
        **kw,
    )


def vspec():
    return pl.BlockSpec(memory_space=pltpu.VMEM)


def hspec():
    return pl.BlockSpec(memory_space=pltpu.HBM)


def sspec():
    return pl.BlockSpec(memory_space=pltpu.SMEM)


def shape(dims, dtype):
    return jax.ShapeDtypeStruct(dims, dtype)


def place(seq_size, quarter, part):
    device = lax.axis_index("rows") * seq_size + lax.axis_index("seq")
    x_bit = (device >> 1) & 1
    y_bit = (device >> 2) & 1
    rest = (device >> 3) * part
    a_mine = x_bit * quarter + y_bit * (quarter // 2) + rest
    b_mine = y_bit * quarter + x_bit * (quarter // 2) + rest
    return (device & 1) == 1, a_mine, b_mine


def three_rows(scorer, rows):
    s1, s2, s3 = split3(scorer.reshape(1, scorer.shape[0]))
    row = lax.broadcasted_iota(jnp.int32, (rows, scorer.shape[0]), 0)
    pick = jnp.where(row == 0, s1.astype(F32), jnp.where(row == 1, s2.astype(F32), s3.astype(F32)))
    return jnp.where(row < 3, pick, 0.0).astype(BF)


def tap_kernel(table_hbm, weight_hbm, hi_ref, lo_ref, table_ref, weight_ref, sem):
    taps = weight_ref.shape[0]
    vocab = table_ref.shape[0]
    copies = [pltpu.make_async_copy(weight_hbm.at[k], weight_ref.at[k], sem.at[k]) for k in range(taps)]
    copies.insert(0, pltpu.make_async_copy(table_hbm, table_ref, sem.at[taps]))
    for copy in copies:
        copy.start()
    copies[0].wait()
    for k in range(taps):
        copies[1 + k].wait()
        hi, lo = split2(dot_nn(table_ref[...], weight_ref[k]))
        hi_ref[k * vocab : (k + 1) * vocab] = hi
        lo_ref[k * vocab : (k + 1) * vocab] = lo


def roll(v, by):
    by = by % v.shape[1]
    return pltpu.roll(v, by, 1) if by else v


def local_kernel(
    calib_ref, mine_ref, from_left_ref, hi_ref, lo_ref, bias_ref, cot_ref,
    scorer_ref, keep_ref, send_ref, ext_ref, idt_ref, band_ref, y_ref, full_q_ref, *, seq_size, taps,
):
    span = keep_ref.shape[0] - HALO
    width = hi_ref.shape[1]
    vocab = hi_ref.shape[0] // taps
    half = width // 2
    own_blocks = span // 2
    lanes = y_ref.shape[0]
    sizes = calib_ref.shape[0]
    front = span
    upper = place(seq_size, 1, 1)[0]
    spare = lax.broadcasted_iota(jnp.int32, (1, lanes - span), 1)

    mine = mine_ref[...].astype(F32)
    length = (256.0 * mine[2:3, 0:1] + mine[3:4, 0:1]).astype(jnp.int32)

    def line_up(at):
        near_left = from_left_ref[:, 2 * span - lanes : span].astype(F32)[at : at + 1]
        rest = jnp.where(spare >= lanes - span - HALO, near_left, 0.0)
        return jnp.concatenate([mine[at : at + 1], rest], axis=1)

    pos = lax.broadcasted_iota(jnp.int32, (1, lanes), 1)
    own = jnp.where(pos < span, 1.0, 0.0)
    place_in_row = lax.axis_index("seq") * span + jnp.where(pos < front, pos, pos - lanes)
    near = (pos < front) | (pos >= lanes - HALO)
    mask = jnp.where(near & (place_in_row >= 0) & (place_in_row < length), 1.0, 0.0)
    seg = line_up(1)
    known = jnp.where(mask > 0.5, line_up(0), -1.0)
    row16 = lax.broadcasted_iota(jnp.int32, (16, span // 2), 0)
    row8 = lax.broadcasted_iota(jnp.int32, (8, lanes), 0)
    idt = jnp.zeros((16, span // 2), F32)
    by_tap = jnp.zeros((8, lanes), F32)
    for k in range(taps):
        moved = roll(known, taps - 1 - k)
        by_tap = jnp.where(row8 == k, moved, by_tap)
        for i in range(2):
            idt = jnp.where(row16 == 2 * k + i, moved[:, i * (span // 2) : (i + 1) * (span // 2)], idt)
        before = pltpu.roll(moved[:, span:lanes], HALO, 1)
        before = jnp.concatenate([before] * (span // 2 // (lanes - span)), axis=1)
        idt = jnp.where(row16 == 2 * taps + k, before, idt)
    idt = idt.astype(BF)
    idt_ref[...] = idt
    column = jnp.transpose(by_tap)
    column = jnp.concatenate([column[0:front], column[lanes - HALO : lanes]], axis=0)
    value = lax.broadcasted_iota(jnp.int32, (front + HALO, vocab), 1).astype(F32)
    one_hot = [jnp.where(column[:, k : k + 1] == value, 1.0, 0.0).astype(BF) for k in range(taps)]
    one_hot = jnp.concatenate(one_hot, axis=1)
    y = dot_nn(one_hot, hi_ref[...]) + dot_nn(one_hot, lo_ref[...])
    y = (y + bias_ref[...].reshape(1, width)).astype(BF)
    y_ref[0:front] = y[0:front]
    y_ref[front : lanes - HALO] = jnp.zeros((lanes - HALO - front, width), BF)
    y_ref[lanes - HALO : lanes] = y[front : front + HALO]
    full_q_ref[0:own_blocks] = cot_ref[0]
    full_q_ref[own_blocks : own_blocks + HALO] = three_rows(scorer_ref[...], HALO)
    tail = own_blocks
    q_rows = own_blocks + HALO
    dots = dot_nt(full_q_ref[...], y_ref[...])
    u = dots[tail : tail + 1] + dots[tail + 1 : tail + 2] + dots[tail + 2 : tail + 3]

    line = lax.broadcasted_iota(jnp.int32, (q_rows, lanes), 0)
    valid, match, grads = [], [], []
    for d in range(sizes):
        valid.append(mask * roll(mask, d) * jnp.where(seg == roll(seg, d), 1.0, 0.0))
        ahead = jnp.where(pos + d >= lanes, pos + d - lanes, pos + d)
        block = jnp.where(ahead < front, lax.shift_right_logical(ahead, 1), -1)
        match.append(line == block)
        picked = jnp.sum(jnp.where(match[d], dots, 0.0), axis=0, keepdims=True)
        grads.append(0.5 * roll(picked, d))
    counted, inv, scores, dprobs = 0.0, [], [], []
    run_u, run_g = 0.0, 0.0
    for d in range(sizes):
        counted = counted + valid[d]
        inv.append(1.0 / jnp.maximum(counted, 1.0))
        run_u = run_u + valid[d] * roll(u, d)
        run_g = run_g + valid[d] * grads[d]
        scores.append(run_u * inv[d])
        dprobs.append(run_g * inv[d])
    logits = [sum(scores[b] * calib_ref[b, c] for b in range(sizes)) for c in range(sizes)]
    top = logits[0]
    for c in range(1, sizes):
        top = jnp.maximum(top, logits[c])
    powers = [jnp.exp(v - top) for v in logits]
    total = sum(powers)
    probs = [v / total for v in powers]
    lse = top + jnp.log(total)
    mean_logit = sum(p * v for p, v in zip(probs, logits))
    mean_grad = sum(p * v for p, v in zip(probs, dprobs))
    entropy = own * mask * (lse - mean_logit)
    parts = [
        [p * (v - mean_grad) for p, v in zip(probs, dprobs)],
        [mask * p * (v - mean_logit) for p, v in zip(probs, logits)],
    ]
    alpha, later = [None] * sizes, 0.0
    for d in reversed(range(sizes)):
        later = later + probs[d] * inv[d]
        alpha[d] = valid[d] * later
    gammas, calibs = [], []
    for part in parts:
        dscores = [sum(part[c] * calib_ref[b, c] for c in range(sizes)) for b in range(sizes)]
        later, gamma = 0.0, 0.0
        for d in reversed(range(sizes)):
            later = later + inv[d] * dscores[d]
            gamma = gamma + roll(own * valid[d] * later, -d)
        gammas.append(gamma)
        calibs.append([[jnp.sum(own * scores[b] * part[c], axis=1, keepdims=True) for c in range(sizes)] for b in range(sizes)])
    band = jnp.where((line >= tail) & (line < tail + 3), gammas[0], 0.0)
    for d in range(sizes):
        band = band + jnp.where(match[d], 0.5 * roll(alpha[d], -d), 0.0)
    band_hi, band_lo = split2(band)
    band_ref[0] = band_hi[0:own_blocks]
    band_ref[1] = band_lo[0:own_blocks]
    dy = dot_tn(band_hi, full_q_ref[...]) + dot_tn(band_lo, full_q_ref[...])
    dy = jnp.concatenate([dy[0:span], dy[lanes - HALO : lanes]], axis=0).astype(BF)
    left, right = dy[:, 0:half], dy[:, half:width]
    keep_ref[...] = jnp.where(upper, right, left)
    send_ref[0 : span + HALO] = jnp.where(upper, left, right)
    grad_bias = jnp.sum(dy.astype(F32), axis=0, keepdims=True)

    row16 = lax.broadcasted_iota(jnp.int32, (16, lanes), 0)
    stack = jnp.zeros((16, lanes), F32)
    pieces = split3(gammas[0]) + split3(gammas[1])
    for i, piece in enumerate(pieces):
        stack = jnp.where(row16 == i, piece.astype(F32), stack)
    stack = stack.astype(BF)
    by_y = dot_nn(stack, y_ref[...])
    grad_scorer = [by_y[3 * i : 3 * i + 1] + by_y[3 * i + 1 : 3 * i + 2] + by_y[3 * i + 2 : 3 * i + 3] for i in range(2)]
    ext_ref[...] = jnp.zeros(ext_ref.shape, F32)
    for i, row in enumerate(grad_scorer + [grad_bias]):
        ext_ref[2 * i : 2 * i + 1] = row[:, 0:half]
        ext_ref[2 * i + 1 : 2 * i + 2] = row[:, half:width]
    by_tap = dot_nn(stack[:, 0:span], one_hot[0:span])
    last = dot_nn(jnp.roll(stack[:, span:lanes], HALO, 1)[:, 0:HALO], one_hot[span : span + HALO])
    by_tap = by_tap[3:4] + by_tap[4:5] + by_tap[5:6] + (last[3:4] + last[4:5] + last[5:6])
    by_tap = jnp.concatenate([by_tap, jnp.zeros((1, 4 * half - taps * vocab), F32)], axis=1)
    for i in range(4):
        ext_ref[6 + i : 7 + i] = by_tap[:, i * half : (i + 1) * half]
    spot = lax.broadcasted_iota(jnp.int32, (1, half), 1)
    misc = jnp.zeros((1, half), F32)
    sums = [calibs[i][b][c] for i in range(2) for b in range(sizes) for c in range(sizes)]
    sums.append(jnp.sum(entropy, axis=1, keepdims=True))
    sums.append(jnp.sum(own * mask, axis=1, keepdims=True))
    sums.append(jnp.sum(gammas[1], axis=1, keepdims=True))
    for i, one in enumerate(sums):
        misc = jnp.where(spot == i, one, misc)
    ext_ref[10:11] = misc
    send_ref[span + HALO : span + HALO + 16] = coded(ext_ref[...])
    send_ref[span + HALO + 16 : span + HALO + 32] = jnp.concatenate([idt, jnp.zeros((16, half - idt.shape[1]), BF)], axis=1)


def mix_kernel(band_ref, y_ref, blocks_ref, token_ref):
    blocks_ref[0] = (dot_nn(band_ref[0], y_ref[...]) + dot_nn(band_ref[1], y_ref[...])).astype(BF)
    token_ref[...] = jnp.zeros(token_ref.shape, F32)


def coded(ext):
    hi = ext.astype(BF).astype(F32)
    lo = ext - hi
    return jnp.concatenate([hi[0:11], lo[0:2], lo[4:6], lo[10:11]], axis=0).astype(BF)


def decoded(code):
    w = code.astype(F32)
    rows = [w[0:2] + w[11:13], w[2:4], w[4:6] + w[13:15], w[6:10], w[10:11] + w[15:16], jnp.zeros((5, w.shape[1]), F32)]
    return jnp.concatenate(rows, axis=0)


def joined(ext_ref):
    return decoded(coded(ext_ref[...]))


def pair(ref, at):
    return decoded(ref[at : at + 16])


def local_value(shape_, dim, a_mine, b_mine, vocab):
    slot = lax.broadcasted_iota(jnp.int32, shape_, dim)
    return jnp.bitwise_xor(slot, jnp.where(slot < vocab // 2, a_mine, b_mine))


def table_kernel(keep_ref, idt_ref, got_ref, ext_ref, a_keep, a_send, b_keep, b_send, ext_out, *, seq_size, part):
    span, half = keep_ref.shape[0] - HALO, keep_ref.shape[1]
    taps, quarter, _ = a_keep.shape
    vocab = 4 * quarter
    _, a_mine, b_mine = place(seq_size, quarter, part)
    value = local_value((vocab, 1), 0, a_mine, b_mine, vocab).astype(F32)
    mine = idt_ref[...].astype(F32)
    theirs = got_ref[span + HALO + 16 : span + HALO + 32].astype(F32)
    wide = mine.shape[1]
    near = lax.broadcasted_iota(jnp.int32, (1, 128), 1) < HALO
    both = jnp.concatenate([keep_ref[span : span + HALO], got_ref[span : span + HALO], jnp.zeros((128 - 2 * HALO, half), BF)], axis=0)
    for k in range(taps):
        at = 2 * taps + k
        row = jnp.where(near, mine[at : at + 1, 0:128], pltpu.roll(theirs[at : at + 1, 0:128], HALO, 1))
        acc = dot_nn(jnp.where(row == value, 1.0, 0.0).astype(BF), both)
        for i in range(span // wide):
            for ids, grad in ((mine, keep_ref), (theirs, got_ref)):
                row = ids[2 * k + i : 2 * k + i + 1, 0:wide]
                one_hot = jnp.where(row == value, 1.0, 0.0).astype(BF)
                term = dot_nn(one_hot, grad[i * wide : (i + 1) * wide])
                acc = acc + term
        a_keep[k] = acc[0:quarter]
        a_send[k * quarter : (k + 1) * quarter] = acc[quarter : 2 * quarter].astype(BF)
        b_keep[k] = acc[2 * quarter : 3 * quarter]
        b_send[k * quarter : (k + 1) * quarter] = acc[3 * quarter : 4 * quarter].astype(BF)
    ext = joined(ext_ref) + pair(got_ref, span + HALO)
    ext_out[...] = ext
    a_send[taps * quarter : taps * quarter + 16] = coded(ext)


def second_kernel(a_in, b_in, a_got, b_got, ext_ref, mixed_ref, order_ref, a_keep, a_send, b_keep, b_send, ext_out):
    del mixed_ref, order_ref
    taps, rows, _ = a_in.shape
    part = rows // 2
    for src, got, keep, send in ((a_in, a_got, a_keep, a_send), (b_in, b_got, b_keep, b_send)):
        for k in range(taps):
            total = src[k] + got[k * rows : (k + 1) * rows].astype(F32)
            keep[k] = total[0:part]
            send[k * part : (k + 1) * part] = total[part:rows].astype(BF)
    ext = joined(ext_ref) + pair(a_got, taps * rows)
    ext_out[...] = ext
    a_send[taps * part : taps * part + 16] = coded(ext)


def third_kernel(a_in, b_in, a_got, b_got, ext_ref, keep, ext_out, *sends):
    taps, rows, _ = a_in.shape
    peers = len(sends)
    part = rows // (peers + 1)
    ext = joined(ext_ref) + pair(a_got, taps * rows)
    ext_out[...] = ext
    groups = 2 * taps
    pieces = [[] for _ in range(peers + 1)]
    for src, got in ((a_in, a_got), (b_in, b_got)):
        for k in range(taps):
            total = src[k] + got[k * rows : (k + 1) * rows].astype(F32)
            for t in range(peers + 1):
                pieces[t].append(total[t * part : (t + 1) * part])
    for t in range(peers + 1):
        block = jnp.concatenate(pieces[t], axis=0)
        if t == 0:
            keep[...] = block
        else:
            send = sends[t - 1]
            send[0 : groups * part] = block.astype(BF)
            send[groups * part : groups * part + 16] = coded(ext)


def tree_sum(items):
    while len(items) > 1:
        items = [items[i] + items[i + 1] for i in range(0, len(items), 2)]
    return items[0]


def shard_kernel(keep, ext_ref, scorer_ref, *refs, seq_size, taps, vocab):
    gots, (shard, loss_ref, bias_ref, grad_scorer_ref, calib_ref) = refs[:-5][::-1], refs[-5:]
    size, half = keep.shape
    part = size // (2 * taps)
    upper, a_mine, b_mine = place(seq_size, vocab // 4, part)
    ext = tree_sum([joined(ext_ref)] + [pair(g, size) for g in gots])
    total = tree_sum([keep[...]] + [g[0:size].astype(F32) for g in gots])
    spot = lax.broadcasted_iota(jnp.int32, (1, half), 1)
    misc = ext[10:11]
    by_tap = jnp.concatenate([ext[i : i + 1] for i in range(6, 10)], axis=1)

    def one(i):
        return jnp.sum(jnp.where(spot == i, misc, 0.0), axis=1, keepdims=True)

    count = one(33)
    scorer = scorer_ref[...].reshape(1, 2 * half)
    mine = jnp.where(upper, scorer[:, half:], scorer[:, :half])
    step = lax.broadcasted_iota(jnp.int32, (part, vocab), 0)
    lane = lax.broadcasted_iota(jnp.int32, (part, vocab), 1)
    pieces = []
    for g in range(2):
        hit = lane == step + (a_mine if g == 0 else vocab // 2 + b_mine)
        for k in range(taps):
            column = jnp.sum(jnp.where(hit, by_tap[:, k * vocab : (k + 1) * vocab], 0.0), axis=1, keepdims=True)
            at = (g * taps + k) * part
            pieces.append(total[at : at + part] - (column / count) * mine)
    shard[...] = jnp.concatenate(pieces, axis=0).astype(BF)

    def whole(i):
        return jnp.concatenate([ext[i : i + 1], ext[i + 1 : i + 2]], axis=1)

    grad_scorer_ref[...] = (whole(0) - whole(2) / count).reshape(2 * half)
    bias_ref[...] = (whole(4) - (one(34) / count) * scorer).reshape(2 * half)
    row = lax.broadcasted_iota(jnp.int32, calib_ref.shape, 0)
    col = lax.broadcasted_iota(jnp.int32, calib_ref.shape, 1)
    out = jnp.zeros(calib_ref.shape, F32)
    for b in range(4):
        for c in range(4):
            out = jnp.where((row == b) & (col == c), one(4 * b + c) - one(16 + 4 * b + c) / count, out)
    calib_ref[...] = out
    loss_ref[...] = one(32) / count


def gather_kernel(*refs, taps):
    shards, (a_ref, b_ref) = refs[:-2], refs[-2:]
    part = shards[0].shape[0] // (2 * taps)
    wide = [s[...].astype(F32) for s in shards]
    for g, out in enumerate((a_ref, b_ref)):
        rows = [w[(g * taps + k) * part : (g * taps + k + 1) * part] for k in range(taps) for w in wide]
        out[...] = jnp.concatenate(rows, axis=0).astype(BF)


def double_kernel(a_ref, b_ref, a_got, b_got, early_ref, a_out, b_out, *, taps):
    rows = a_ref.shape[0] // taps
    for g, (src, got, out) in enumerate(((a_ref, a_got, a_out), (b_ref, b_got, b_out))):
        for k in range(taps):
            at = 2 * rows * k
            for first, ref in ((at, src), (at + rows, got)):
                piece = ref[k * rows : (k + 1) * rows]
                out[first : first + rows] = piece
                early_ref[g, first : first + rows] = piece


def order_kernel(table_ref, after_ref, out_ref, token_ref, *, seq_size, part):
    del after_ref
    token_ref[...] = jnp.zeros(token_ref.shape, F32)
    vocab = table_ref.shape[0]
    _, a_mine, b_mine = place(seq_size, vocab // 4, part)
    value = local_value((1, vocab), 1, a_mine, b_mine, vocab)
    natural = lax.broadcasted_iota(jnp.int32, (vocab, vocab), 0)
    out_ref[...] = dot_tn(table_ref[...], jnp.where(natural == value, 1.0, 0.0).astype(BF)).astype(BF)


def final_kernel(
    early, a_late, b_late, far_early, far_a, far_b, table_t_ref, weight_ref, conv_ref, table_ref, buffer, sem, *, seq_size, part,
):
    taps, width, _ = weight_ref.shape
    vocab = table_t_ref.shape[1]
    quarter = vocab // 4
    upper, a_mine, b_mine = place(seq_size, quarter, part)

    def rows_of(k):
        at = k * quarter
        near = [early[0, at : at + quarter], a_late[at : at + quarter], early[1, at : at + quarter], b_late[at : at + quarter]]
        far = [far_early[0, at : at + quarter], far_a[at : at + quarter], far_early[1, at : at + quarter], far_b[at : at + quarter]]
        near, far = jnp.concatenate(near, axis=0), jnp.concatenate(far, axis=0)
        return jnp.concatenate([jnp.where(upper, far, near), jnp.where(upper, near, far)], axis=1)

    rows = []
    for k in range(taps):
        rows.append(rows_of(k))
        buffer[k] = dot_nn(table_t_ref[...], rows[k])
        pltpu.make_async_copy(buffer.at[k], conv_ref.at[k], sem.at[k]).start()
    acc = 0.0
    for k in range(taps):
        acc = acc + dot_nt(weight_ref[k], rows[k])
    acc = jnp.transpose(acc)
    for at in range(0, vocab, part):
        to = (at ^ a_mine) if at < vocab // 2 else vocab // 2 + ((at - vocab // 2) ^ b_mine)
        table_ref[pl.ds(pl.multiple_of(to, part), part)] = acc[at : at + part]
    for k in range(taps):
        pltpu.make_async_copy(buffer.at[k], conv_ref.at[k], sem.at[k]).wait()


def neighbour(shard, axis, by):
    length = lax.axis_size(axis)
    return lax.ppermute(shard, axis, [(i, i + by) for i in range(length) if 0 <= i + by < length])


def swap(shard, flip, count):
    return lax.ppermute(shard, AXES, [(i, i ^ flip) for i in range(count)])


def body(
    byte_ids, seg_ids, row_len, embed_table, conv_weight, conv_bias, scorer, calibration, cotangent
):
    row_count, span = byte_ids.shape
    vocab, width = embed_table.shape
    taps = conv_weight.shape[0]
    half = width // 2
    quarter = vocab // 4
    seq_size = lax.axis_size("seq")
    count = lax.axis_size("rows") * seq_size
    depth = count // 8
    assert row_count == 1 and vocab == 256 and taps == 5 and calibration.shape == (4, 4)
    assert seq_size % 2 == 0 and depth >= 1 and quarter // 2 % depth == 0
    part = quarter // 2 // depth
    eighth = quarter // 2
    size = 2 * taps * part
    lanes = span + 128

    row = lax.broadcasted_iota(jnp.int32, (HALO, span), 0)
    digit = jnp.where(row == 2, lax.shift_right_logical(row_len[0], 8), row_len[0] & 255)
    to_right = jnp.where(row == 0, byte_ids, jnp.where(row == 1, seg_ids, digit)).astype(BF)
    from_left = neighbour(to_right, "seq", 1)

    hi, lo = pl.pallas_call(
        tap_kernel,
        out_shape=(shape((taps * vocab, width), BF),) * 2,
        name="taps",
        in_specs=[hspec()] * 2,
        out_specs=(vspec(),) * 2,
        scratch_shapes=[
            pltpu.VMEM((vocab, width), BF),
            pltpu.VMEM((taps, width, width), BF),
            pltpu.SemaphoreType.DMA((taps + 1,)),
        ],
        compiler_params=pltpu.CompilerParams(vmem_limit_bytes=TAPS_LIMIT),
    )(embed_table, conv_weight)

    keep, send, ext, idt, band, y = call(
        functools.partial(local_kernel, seq_size=seq_size, taps=taps),
        (
            shape((span + HALO, half), BF),
            shape((span + HALO + 32, half), BF),
            shape((16, half), F32),
            shape((16, span // 2), BF),
            shape((2, span // 2, lanes), BF),
            shape((lanes, width), BF),
        ),
        "local",
        in_specs=[sspec()] + [vspec()] * 7,
        out_specs=(vspec(),) * 6,
        scratch_shapes=[pltpu.VMEM((span // 2 + HALO, width), BF)],
    )(calibration, to_right, from_left, hi, lo, conv_bias, cotangent, scorer)

    got = swap(send, 1, count)
    a_keep, a_send, b_keep, b_send, ext = call(
        functools.partial(table_kernel, seq_size=seq_size, part=part),
        (
            shape((taps, quarter, half), F32),
            shape((taps * quarter + 16, half), BF),
            shape((taps, quarter, half), F32),
            shape((taps * quarter, half), BF),
            shape((16, half), F32),
        ),
        "by_value",
        in_specs=[vspec()] * 4,
        out_specs=(vspec(),) * 5,
    )(keep, idt, got, ext)
    token = shape((8, 128), F32)
    blocks, mixed = call(
        mix_kernel,
        (shape((1, span // 2, width), BF), token),
        "mix",
        in_specs=[vspec()] * 2,
        out_specs=(vspec(),) * 2,
    )(band, y)
    table_t, ordered = call(
        functools.partial(order_kernel, seq_size=seq_size, part=part),
        (shape((width, vocab), BF), token),
        "order",
        in_specs=[vspec()] * 2,
        out_specs=(vspec(),) * 2,
    )(embed_table, ext)

    a_got, b_got = swap(a_send, 2, count), swap(b_send, 4, count)
    a_keep, a_send, b_keep, b_send, ext = call(
        second_kernel,
        (
            shape((taps, eighth, half), F32),
            shape((taps * eighth + 16, half), BF),
            shape((taps, eighth, half), F32),
            shape((taps * eighth, half), BF),
            shape((16, half), F32),
        ),
        "second",
        in_specs=[vspec()] * 7,
        out_specs=(vspec(),) * 5,
    )(a_keep, b_keep, a_got, b_got, ext, mixed, ordered)

    a_got, b_got = swap(a_send, 4, count), swap(b_send, 2, count)
    outs = call(
        third_kernel,
        (shape((size, half), F32), shape((16, half), F32)) + (shape((size + 16, half), BF),) * (depth - 1),
        "third",
        in_specs=[vspec()] * 5,
        out_specs=(vspec(),) * (depth + 1),
    )(a_keep, b_keep, a_got, b_got, ext)
    mine, ext, sends = outs[0], outs[1], outs[2:]
    gots = [swap(s, 8 * (t + 1), count) for t, s in enumerate(sends)]
    shard, loss, grad_bias, grad_scorer, grad_calib = call(
        functools.partial(shard_kernel, seq_size=seq_size, taps=taps, vocab=vocab),
        (shape((size, half), BF), shape((1, 1), F32), shape((width,), F32), shape((width,), F32), shape((4, 4), F32)),
        "shard",
        in_specs=[vspec()] * (3 + len(gots)),
        out_specs=(vspec(),) * 5,
    )(mine, ext, scorer, *gots[::-1])

    gathered = [shard] + [swap(shard, 8 * t, count) for t in range(1, depth)]
    a_out, b_out = call(
        functools.partial(gather_kernel, taps=taps),
        (shape((taps * eighth, half), BF),) * 2,
        "gather",
        in_specs=[vspec()] * depth,
        out_specs=(vspec(),) * 2,
    )(*gathered)
    a_got, b_got = swap(a_out, 4, count), swap(b_out, 2, count)
    early, a_out, b_out = call(
        functools.partial(double_kernel, taps=taps),
        (shape((2, taps * quarter, half), BF),) + (shape((taps * quarter, half), BF),) * 2,
        "double",
        in_specs=[vspec()] * 4,
        out_specs=(vspec(),) * 3,
    )(a_out, b_out, a_got, b_got)
    a_late, b_late = swap(a_out, 2, count), swap(b_out, 4, count)
    far_early = swap(early, 1, count)
    far_a, far_b = swap(a_late, 1, count), swap(b_late, 1, count)

    conv, grad_table = call(
        functools.partial(final_kernel, seq_size=seq_size, part=part),
        (shape((taps, width, width), F32), shape((vocab, width), F32)),
        "final",
        in_specs=[vspec()] * 8,
        out_specs=(hspec(), vspec()),
        scratch_shapes=[
            pltpu.VMEM((taps, width, width), F32),
            pltpu.SemaphoreType.DMA((taps,)),
        ],
    )(early, a_late, b_late, far_early, far_a, far_b, table_t, conv_weight)
    return (blocks, loss.reshape(()), grad_table, conv, grad_bias, grad_scorer, grad_calib)


def solution(mesh):
    return jax.shard_map(
        body,
        mesh=mesh,
        in_specs=(
            P("rows", "seq"),
            P("rows", "seq"),
            P("rows"),
            P(),
            P(),
            P(),
            P(),
            P(),
            P("rows", "seq", None),
        ),
        out_specs=(P("rows", "seq", None), P(), P(), P(), P(), P(), P()),
        check_vma=False,
    )
```
